1024 devices in a mesh: dom: 16 (over x_hi, y, core), fsdp: 64 (over z, x_lo).
Axes of the slice: x: 4 (x_hi: 2, x_lo: 2; x = x_hi * 2 + x_lo), y: 4, z: 32, core: 2. Of those that a mesh axis runs over, the one named last changes fastest.
Arguments:
- tokens: bfloat16 [262144, 1536], P(('dom', 'fsdp')), may hold values from -24 to 24
- gain: bfloat16 [1536], P('fsdp'), may hold values from 0.099609375 to 1.8984375
- kv_weight: bfloat16 [1536, 512], P('fsdp'), may hold values from -0.15625 to 0.15625
- positions: int32 [262144], P(('dom', 'fsdp')), may hold values from 0 to 4095
- cotangent: bfloat16 [262144, 512], P(('dom', 'fsdp')), may hold values from -6 to 6
- counts: int32 [16, 64], replicated, may hold values from 0 to 2, as said below
- ratios: int32 [16], replicated, may hold values from 1 to 8
Outputs:
- keys_values: bfloat16 [262144, 512], P(('dom', 'fsdp'))
- weight_grad: float32 [1536, 512], P('fsdp')
- gain_grad: float32 [1536], P('fsdp')
The draws below stay inside these ranges and needn't reach their ends.
Inputs may be any that keep to these rules, and one draw needn't show every extreme that they name: counts gives each device's live rows in blocks of 128; every domain has a device with one or more live blocks, and some device holds 2 live blocks in every draw.
All inputs are finite; a program needn't handle non-finite values.
Results may differ from the reference program's by a relative error of at most 0.0051.
Values may be sent and summed in bfloat16 or wider, within the bound.
A program may use at most 32 MiB of HBM per device.

```python
import jax
import jax.numpy as jnp
from jax import lax

D = 1536
KVH = 2
HD = 128
BLOCK = 128
BLK = 2
ROWS_DEV = 256
DOMAINS = 16
GROUP = 64
TOKENS = 262144


def draw_counts(key, part):
    keys = jax.random.split(key, 5)
    levels = jax.random.randint(keys[0], (DOMAINS, 1), 1, BLK + 1)
    raw = jax.random.randint(keys[1], (DOMAINS, GROUP), 0, 1048576)
    blocks = raw % (levels + 1)
    anchor = jax.random.randint(keys[2], (DOMAINS, 1), 0, GROUP)
    anchored = jnp.arange(GROUP)[None, :] == anchor
    blocks = jnp.where(anchored, jnp.maximum(blocks, 1), blocks)
    domain_pick = jax.random.randint(keys[3], (), 0, DOMAINS)
    member_pick = jax.random.randint(keys[4], (), 0, GROUP)
    chosen = (jnp.arange(DOMAINS)[:, None] == domain_pick) & (jnp.arange(GROUP)[None, :] == member_pick)
    return jnp.where(chosen, BLK, blocks).astype(jnp.int32)


def set_ends(result, own_key, least, high):
    longest = result.shape.index(max(result.shape))
    spots = []
    for shift in (0, 1):
        where = [jax.random.randint(jax.random.fold_in(own_key, axis), (), 0, length) for axis, length in enumerate(result.shape)]
        where[longest] = (where[longest] + shift) % result.shape[longest]
        spots.append(tuple(where))
    return result.at[spots[0]].set(least).at[spots[1]].set(high)


def with_spikes(entries, stream_key, source, target, shards_of, factor):
    def block_of(axis_at):
        return (jnp.arange(entries.shape[axis_at]) // (entries.shape[axis_at] // shards_of)).reshape((-1,) + (1,) * (entries.ndim - 1 - axis_at))

    one_side = jax.random.permutation(stream_key, shards_of)[block_of(target)]
    far = (block_of(target) + shards_of // 2) % shards_of
    return jnp.where((block_of(source) == one_side) | (block_of(source) == far), factor * entries, entries)


def block_scale(key, extent, shards, low, high):
    level = 1.0
    for axis_at, shards_of in shards:
        heights = jax.random.uniform(jax.random.fold_in(jax.random.fold_in(key, 6), axis_at), (shards_of,), jnp.float32, low / len(shards), high / len(shards))
        level = level * jnp.repeat(jnp.exp(heights), extent[axis_at] // shards_of).reshape((-1,) + (1,) * (len(extent) - 1 - axis_at))
    return level


def bell_draw(rng, shape, spread, most, cuts=(), kind=jnp.bfloat16):
    entries = jax.random.normal(rng, shape, jnp.float32) * spread
    if len(cuts) > 0:
        entries = block_scale(rng, shape, cuts, -0.22, 0.18) * entries
    return jnp.clip(entries, min=-most, max=most).astype(kind)


def heavy_noise(stream_key, dims, deviation, most, cuts, heavy, kind=jnp.bfloat16):
    entries = deviation * jax.random.normal(stream_key, dims, jnp.float32)
    if cuts:
        entries = entries * block_scale(stream_key, dims, cuts, -0.22, 0.18)
    return jnp.clip(with_spikes(entries, jax.random.fold_in(stream_key, 3), *heavy), -most, most).astype(kind)


def setup_inputs(seed: int = 0) -> dict:
    seeds = jax.random.split(jax.random.key(seed), 8)
    tokens = heavy_noise(seeds[0], (TOKENS, D), 1.0, 24.0, ((0, 1024),), (0, 1, 512, 6.0))
    gain = jnp.clip(1.0 + 0.18 * jax.random.normal(seeds[1], (D,), jnp.float32), 0.099609375, 1.8984375).astype(jnp.bfloat16)
    kv_weight = bell_draw(seeds[2], (D, 2 * KVH * HD), D ** -0.5, 0.15625, ((0, 64),))
    positions = set_ends(jax.random.randint(seeds[3], (TOKENS,), 0, 4096), jax.random.fold_in(seeds[3], 1), 0, 4095).astype(jnp.int32)
    cotangent = bell_draw(seeds[4], (TOKENS, 2 * KVH * HD), 1.0, 6.0, ((0, 1024),))
    counts = draw_counts(jax.random.fold_in(seeds[7], 71), 0)
    ratios = set_ends(jax.random.randint(seeds[6], (DOMAINS,), 1, 9), jax.random.fold_in(seeds[6], 1), 1, 8).astype(jnp.int32)
    return dict(tokens=tokens, gain=gain, kv_weight=kv_weight, positions=positions, cotangent=cotangent, counts=counts, ratios=ratios)


def rotary_tables(position_ids, half_width, head_size):
    exponents = jnp.arange(half_width, dtype=jnp.float32) * (2.0 / head_size)
    frequency = jnp.power(jnp.float32(1000000.0), -exponents)
    angles = position_ids.astype(jnp.float32)[:, None] * frequency[None, :]
    return (jnp.cos(angles)[:, None, :], jnp.sin(angles)[:, None, :])

def rotate_heads(values, cosines, sines, heads, head_size, direction):
    rows = values.shape[0]
    half_width = head_size // 2
    shaped = values.reshape(rows, heads, head_size)
    first = shaped[:, :, :half_width]
    second = shaped[:, :, half_width:]
    turned = jnp.concatenate([first * cosines - direction * second * sines, second * cosines + direction * first * sines], axis=2)
    return turned.reshape(rows, heads * head_size)

def normalize(token_rows, gain):
    token_float = token_rows.astype(jnp.float32)
    mean_square = lax.optimization_barrier(jnp.mean(token_float * token_float, axis=1, keepdims=True))
    normed = token_float * lax.rsqrt(mean_square + 1e-06)
    scaled = (normed * gain.astype(jnp.float32)[None, :]).astype(jnp.bfloat16)
    return (normed, scaled)

def reference(tokens, gain, kv_weight, positions, cotangent, counts, ratios):
    devices_all = DOMAINS * GROUP
    key_width = KVH * HD
    domain_rows = (BLOCK * lax.optimization_barrier(jnp.sum(counts, axis=1))).astype(jnp.float32)
    live_total = jnp.sum(domain_rows)
    ratio_float = ratios.astype(jnp.float32)
    factor = ratio_float / jnp.sum(ratio_float) * live_total / domain_rows
    row_ids = jnp.arange(ROWS_DEV, dtype=jnp.int32)

    def one_device(running, inputs):
        token_rows, position_ids, cot_rows, device = inputs
        domain_index = device // GROUP
        member = device % GROUP
        normed, scaled = normalize(token_rows, gain)
        projected = jnp.dot(scaled, kv_weight, preferred_element_type=jnp.float32)
        cosines, sines = rotary_tables(position_ids, HD // 2, HD)
        keys_out = jnp.concatenate([rotate_heads(projected[:, :key_width], cosines, sines, KVH, HD, 1.0), projected[:, key_width:]], axis=1).astype(jnp.bfloat16)
        live_rows = row_ids < BLOCK * counts[domain_index, member]
        row_factor = jnp.where(live_rows, factor[domain_index], jnp.float32(0.0))
        weighted = cot_rows.astype(jnp.float32) * row_factor[:, None]
        upstream = jnp.concatenate([rotate_heads(weighted[:, :key_width], cosines, sines, KVH, HD, -1.0), weighted[:, key_width:]], axis=1).astype(jnp.bfloat16)
        weight_term = jnp.dot(scaled.T, upstream, preferred_element_type=jnp.float32)
        scaled_grad = jnp.dot(upstream, kv_weight.T, preferred_element_type=jnp.float32)
        gain_term = lax.optimization_barrier(jnp.sum(scaled_grad * normed, axis=0))
        return ((running[0] + weight_term, running[1] + gain_term), keys_out)
    initial = (jnp.zeros((D, 2 * key_width), jnp.float32), jnp.zeros((D,), jnp.float32))
    inputs = (tokens.reshape(devices_all, ROWS_DEV, D), positions.reshape(devices_all, ROWS_DEV), cotangent.reshape(devices_all, ROWS_DEV, 2 * key_width), jnp.arange(devices_all, dtype=jnp.int32))
    sums, outputs = lax.scan(one_device, initial, inputs)
    root = jnp.sqrt(live_total)
    return (outputs.reshape(TOKENS, 2 * key_width), sums[0] / root, sums[1] / root)
```

```python
import functools

import jax
import jax.numpy as jnp
import numpy as np
from jax import lax
from jax.experimental import pallas as pl
from jax.experimental.pallas import tpu as pltpu
from jax.sharding import PartitionSpec as P

HD = 128
HALF = HD // 2
BLOCK = 128
LANES = 128
MESH = pl.DeviceIdType.MESH
F32 = jnp.float32
BF16 = jnp.bfloat16


def to_column(row, size):
    eye = lax.broadcasted_iota(jnp.int32, (size, size), 0) == lax.broadcasted_iota(
        jnp.int32, (size, size), 1
    )
    return jnp.sum(jnp.where(eye, row, jnp.float32(0.0)), axis=1, keepdims=True)


def to_row(column, size):
    eye = lax.broadcasted_iota(jnp.int32, (size, size), 0) == lax.broadcasted_iota(
        jnp.int32, (size, size), 1
    )
    return jnp.sum(jnp.where(eye, column, jnp.float32(0.0)), axis=0, keepdims=True)


def kernel(
    ny,
    nz,
    counts_ref,
    ratios_ref,
    gain_ref,
    weight_ref,
    positions_ref,
    freq_ref,
    tokens_ref,
    cot_ref,
    kv_ref,
    wg_ref,
    gg_ref,
    own_gw,
    land_g1,
    piece_g,
    full_gw,
    part_m,
    land_r0,
    sum_r0,
    land_r1,
    sum_r1,
    land_r2,
    sum_r2,
    land_r3,
    upstream,
    sem_g1s,
    sem_g1r,
    sem_g2s,
    sem_g2r,
    sem_g3s,
    sem_g3r,
    sem_r0s,
    sem_r0r,
    sem_r1s,
    sem_r1r,
    sem_r2s,
    sem_r2r,
    sem_r3s,
    sem_r3r,
):
    dom = lax.axis_index("dom")
    fsdp = lax.axis_index("fsdp")
    core = lax.rem(dom, 2)
    y = lax.rem(dom // 2, ny)
    x_hi = dom // (2 * ny)
    z = fsdp // 2
    x_lo = lax.rem(fsdp, 2)
    x = x_hi * 2 + x_lo
    q = x_hi * 2 + core
    jn = nz // 8
    rows = tokens_ref.shape[0]
    shard = weight_ref.shape[0]
    cols = weight_ref.shape[1]
    slab = 2 * shard
    key_width = cols // 2
    heads = key_width // HD
    width = tokens_ref.shape[1]
    group = 8 * slab
    lo_own = lax.rem(z + core, 2)
    lo_sib = 1 - lo_own

    def dev(xx, yy, cc, zz):
        return ((xx // 2 * ny + yy) * 2 + cc, zz * 2 + lax.rem(xx, 2))

    def lane_tile(i):
        return pl.ds(pl.multiple_of(i * LANES, LANES), LANES)

    barrier = pltpu.get_barrier_semaphore()

    def greet_plane(i, carry):
        xx = lax.rem(x + i // (2 * ny), 4)
        yy = lax.rem(y + lax.rem(i // 2, ny), ny)
        cc = lax.rem(core + lax.rem(i, 2), 2)
        pl.semaphore_signal(barrier, inc=1, device_id=dev(xx, yy, cc, z), device_id_type=MESH)
        return carry

    lax.fori_loop(1, 8 * ny, greet_plane, 0)

    steps = nz // 4

    def z_peers(s, sign):
        dist = q + 4 * s
        return lax.rem(z + sign * dist + 2 * nz, nz)

    def greet_z(i, carry):
        s, half = i // 2, lax.rem(i, 2)
        for sign in (1, -1):
            zz = z_peers(s, sign)

            @pl.when(zz != z)
            def _():
                pl.semaphore_signal(
                    barrier,
                    inc=1,
                    device_id=dev(x_hi * 2 + half, y, core, zz),
                    device_id_type=MESH,
                )

        return carry

    lax.fori_loop(0, 2 * steps, greet_z, 0)

    gain_col = to_column(gain_ref[...].astype(F32), shard)
    weight = weight_ref[...].astype(F32)
    own_gw[...] = (weight * gain_col).astype(BF16)

    n_self = jnp.where(lax.rem(q, 4) == 0, 4, 0)
    pl.semaphore_wait(barrier, 8 * ny - 1 + 4 * steps - n_self)

    def g1_copy(s):
        far = z_peers(s, 1)
        half = lax.rem(s, 2)
        return (
            far,
            half,
            pltpu.make_async_remote_copy(
                src_ref=own_gw.at[:, lane_tile(y)],
                dst_ref=land_g1.at[s // 2, x_lo],
                send_sem=sem_g1s.at[s],
                recv_sem=sem_g1r.at[s // 2, x_lo],
                device_id=dev(x_hi * 2 + half, y, core, far),
                device_id_type=MESH,
            ),
        )

    def g1_local():
        return pltpu.make_async_copy(
            own_gw.at[:, lane_tile(y)], land_g1.at[0, x_lo], sem_g1r.at[0, x_lo]
        )

    def is_self(far, half):
        return (far == z) & (half == x_lo)

    def g1_start(s, carry):
        far, half, copy = g1_copy(s)

        @pl.when(jnp.logical_not(is_self(far, half)))
        def _():
            copy.start()

        @pl.when(is_self(far, half))
        def _():
            g1_local().start()

        return carry

    lax.fori_loop(0, steps, g1_start, 0)

    counts = counts_ref[...].astype(F32)
    n_dom, n_mem = counts.shape
    domain_rows = BLOCK * jnp.sum(counts, axis=1, keepdims=True)
    live_total = jnp.sum(domain_rows, axis=0, keepdims=True)
    ratio = to_column(ratios_ref[...].astype(F32), n_dom)
    factor = ratio / jnp.sum(ratio, axis=0, keepdims=True) * live_total / domain_rows
    dom_ids = lax.broadcasted_iota(jnp.int32, (n_dom, 1), 0)
    own_factor = jnp.sum(jnp.where(dom_ids == dom, factor, 0.0), axis=0, keepdims=True)
    at_dom = lax.broadcasted_iota(jnp.int32, (n_dom, n_mem), 0) == dom
    at_mem = lax.broadcasted_iota(jnp.int32, (n_dom, n_mem), 1) == fsdp
    own_count = jnp.sum(
        jnp.sum(jnp.where(at_dom & at_mem, counts, 0.0), axis=1, keepdims=True),
        axis=0,
        keepdims=True,
    )
    row_ids = lax.broadcasted_iota(jnp.int32, (rows, 1), 0).astype(F32)
    row_factor = jnp.where(row_ids < BLOCK * own_count, own_factor, 0.0)

    token = tokens_ref[...].astype(F32)
    mean_square = jnp.sum(token * token, axis=1, keepdims=True) * (1.0 / width)
    inv_norm = lax.rsqrt(mean_square + 1e-06)

    pos = positions_ref[...].astype(F32)
    pos_col = jnp.concatenate(
        [to_column(pos[i : i + 1, :], LANES) for i in range(rows // LANES)], axis=0
    )
    angles = pos_col * freq_ref[...]
    cosines = jnp.cos(angles)
    lane_ids = lax.broadcasted_iota(jnp.int32, (rows, HD), 1)
    sines = jnp.where(lane_ids < HALF, -1.0, 1.0) * jnp.sin(angles)

    scale = row_factor * inv_norm
    for h in range(2 * heads):
        part = cot_ref[:, h * HD : (h + 1) * HD].astype(F32) * scale
        if h < heads:
            part = part * cosines - pltpu.roll(part, HALF, 1) * sines
        upstream[:, h * HD : (h + 1) * HD] = part.astype(BF16)

    def m_step(j, carry):
        lhs = tokens_ref[:, pl.ds(pl.multiple_of(j * group, group), group)]
        prod = lax.dot_general(
            lhs, upstream[...], (((0,), (0,)), ((), ())), preferred_element_type=F32
        )
        part_m[j] = prod.reshape(4, 2, slab, cols).astype(BF16)
        return carry

    lax.fori_loop(0, jn, m_step, 0)

    sibling = dev(x, y, 1 - core, z)
    r0 = pltpu.make_async_remote_copy(
        src_ref=part_m.at[:, :, lo_sib],
        dst_ref=land_r0,
        send_sem=sem_r0s,
        recv_sem=sem_r0r,
        device_id=sibling,
        device_id_type=MESH,
    )
    r0.start()

    own_class = q + 4 * x_lo
    r_gather = lax.rem(z - own_class + 2 * nz, 8)

    def g1_arrive(j, carry):
        for half in range(2):
            pltpu.make_async_copy(
                land_g1.at[j, half], land_g1.at[j, half], sem_g1r.at[j, half]
            ).wait()
        at = lax.rem(z - own_class - 8 * j + 2 * nz, nz) // 8
        both = jnp.concatenate(
            [land_g1[j, 0].astype(F32), land_g1[j, 1].astype(F32)], axis=0
        )
        piece_g[at] = both.astype(BF16)
        return carry

    lax.fori_loop(0, jn, g1_arrive, 0)

    r0.wait_recv()

    def r0_sum(i, carry):
        j, hi = i // 4, lax.rem(i, 4)
        total = part_m[j, hi, lo_own].astype(F32) + land_r0[j, hi].astype(F32)
        sum_r0[j, hi] = total.astype(BF16)
        return carry

    lax.fori_loop(0, 4 * jn, r0_sum, 0)

    def r1_copy(k):
        xx = lax.rem(x + k // ny, 4)
        yy = lax.rem(y + lax.rem(k, ny), ny)
        to_class = (xx // 2) * 2 + core + 4 * lax.rem(xx, 2)
        hi = lax.rem(z + to_class, 8) // 2
        return pltpu.make_async_remote_copy(
            src_ref=sum_r0.at[:, hi, :, lane_tile(yy)],
            dst_ref=land_r1.at[k],
            send_sem=sem_r1s.at[k],
            recv_sem=sem_r1r.at[k],
            device_id=dev(xx, yy, core, z),
            device_id_type=MESH,
        )

    def r1_start(k, carry):
        r1_copy(k).start()
        return carry

    lax.fori_loop(1, 4 * ny, r1_start, 0)

    hi_gather = r_gather // 2

    def g2_copy(k):
        xx = lax.rem(x + k // ny, 4)
        yy = lax.rem(y + lax.rem(k, ny), ny)
        return pltpu.make_async_remote_copy(
            src_ref=piece_g,
            dst_ref=full_gw.at[:, hi_gather, lo_own, :, lane_tile(y)],
            send_sem=sem_g2s.at[k],
            recv_sem=sem_g2r.at[k],
            device_id=dev(xx, yy, core, z),
            device_id_type=MESH,
        )

    g2_local = pltpu.make_async_copy(
        piece_g, full_gw.at[:, hi_gather, lo_own, :, lane_tile(y)], sem_g2r.at[0]
    )
    g2_local.start()

    def g2_start(k, carry):
        g2_copy(k).start()
        return carry

    lax.fori_loop(1, 4 * ny, g2_start, 0)

    hi_reduce = lax.rem(z + own_class, 8) // 2
    total1 = sum_r0[:, hi_reduce, :, lane_tile(y)].astype(F32)

    def r1_arrive(k, total):
        r1_copy(k).wait_recv()
        return total + land_r1[k].astype(F32)

    total1 = lax.fori_loop(1, 4 * ny, r1_arrive, total1)
    for half in range(2):
        sum_r1[:, half] = total1[:, half * shard : (half + 1) * shard, :].astype(BF16)

    def r2_copy(i):
        j, half = i // 2, lax.rem(i, 2)
        s = 2 * j + x_lo
        far = z_peers(s, 1)
        return (
            far,
            half,
            s,
            pltpu.make_async_remote_copy(
                src_ref=sum_r1.at[far // 8, half],
                dst_ref=land_r2.at[s],
                send_sem=sem_r2s.at[i],
                recv_sem=sem_r2r.at[s],
                device_id=dev(x_hi * 2 + half, y, core, far),
                device_id_type=MESH,
            ),
        )

    def r2_local():
        return pltpu.make_async_copy(
            sum_r1.at[z // 8, x_lo], land_r2.at[0], sem_r2r.at[0]
        )

    def r2_start(i, carry):
        far, half, s, copy = r2_copy(i)

        @pl.when(jnp.logical_not(is_self(far, half)))
        def _():
            copy.start()

        @pl.when(is_self(far, half))
        def _():
            r2_local().start()

        return carry

    lax.fori_loop(0, steps, r2_start, 0)

    g2_local.wait()

    def g2_arrive(k, carry):
        g2_copy(k).wait_recv()
        return carry

    lax.fori_loop(1, 4 * ny, g2_arrive, 0)
    g3 = pltpu.make_async_remote_copy(
        src_ref=full_gw.at[:, :, lo_own],
        dst_ref=full_gw.at[:, :, lo_own],
        send_sem=sem_g3s,
        recv_sem=sem_g3r,
        device_id=sibling,
        device_id_type=MESH,
    )
    g3.start()

    def r2_arrive(s, total):
        pltpu.make_async_copy(land_r2.at[s], land_r2.at[s], sem_r2r.at[s]).wait()
        return total + land_r2[s].astype(F32)

    sum_r2[...] = lax.fori_loop(
        0, steps, r2_arrive, jnp.zeros((shard, LANES), F32)
    )

    def r3_copy(i):
        hh = lax.rem(x_hi + i // (2 * ny), 2)
        yy = lax.rem(y + lax.rem(i // 2, ny), ny)
        cc = lax.rem(core + lax.rem(i, 2), 2)
        return pltpu.make_async_remote_copy(
            src_ref=sum_r2,
            dst_ref=land_r3.at[q, :, lane_tile(y)],
            send_sem=sem_r3s.at[i],
            recv_sem=sem_r3r.at[i],
            device_id=dev(hh * 2 + x_lo, yy, cc, z),
            device_id_type=MESH,
        )

    r3_local = pltpu.make_async_copy(
        sum_r2, land_r3.at[q, :, lane_tile(y)], sem_r3r.at[0]
    )
    r3_local.start()

    def r3_start(i, carry):
        r3_copy(i).start()
        return carry

    lax.fori_loop(1, 4 * ny, r3_start, 0)

    pltpu.make_async_remote_copy(
        src_ref=full_gw.at[:, :, lo_sib],
        dst_ref=full_gw.at[:, :, lo_sib],
        send_sem=sem_g3s,
        recv_sem=sem_g3r,
        device_id=sibling,
        device_id_type=MESH,
    ).wait_recv()

    def p_step(j, total):
        lhs = tokens_ref[:, pl.ds(pl.multiple_of(j * group, group), group)]
        rhs = full_gw[j].reshape(group, cols)
        return total + jnp.dot(lhs, rhs, preferred_element_type=F32)

    projected = lax.fori_loop(0, jn, p_step, jnp.zeros((rows, cols), F32))
    projected = projected * inv_norm
    for h in range(2 * heads):
        part = projected[:, h * HD : (h + 1) * HD]
        if h < heads:
            part = part * cosines + pltpu.roll(part, HALF, 1) * sines
        kv_ref[:, h * HD : (h + 1) * HD] = part.astype(BF16)

    r3_local.wait()

    def r3_arrive(i, carry):
        r3_copy(i).wait_recv()
        return carry

    lax.fori_loop(1, 4 * ny, r3_arrive, 0)
    total = land_r3[0] + land_r3[1] + land_r3[2] + land_r3[3]
    root = jnp.sqrt(live_total)
    wg_ref[...] = total * gain_col / root
    gain_sum = jnp.sum(total * weight, axis=1, keepdims=True)
    gg_ref[...] = to_row(gain_sum / root, shard)

    def g1_drain(s, carry):
        far, half, copy = g1_copy(s)

        @pl.when(jnp.logical_not(is_self(far, half)))
        def _():
            copy.wait_send()

        return carry

    def r2_drain(i, carry):
        far, half, s, copy = r2_copy(i)

        @pl.when(jnp.logical_not(is_self(far, half)))
        def _():
            copy.wait_send()

        return carry

    def drain(k, carry):
        r1_copy(k).wait_send()
        g2_copy(k).wait_send()
        r3_copy(k).wait_send()
        return carry

    lax.fori_loop(0, steps, g1_drain, 0)
    lax.fori_loop(0, steps, r2_drain, 0)
    lax.fori_loop(1, 4 * ny, drain, 0)
    r0.wait_send()
    g3.wait_send()


def body(ny, nz, tokens, gain, kv_weight, positions, cotangent, counts, ratios):
    rows, width = tokens.shape
    shard, cols = kv_weight.shape
    jn, steps, plane = nz // 8, nz // 4, 4 * ny
    slab = 2 * shard
    exponents = np.arange(HALF) * (2.0 / HD)
    freq = np.power(1000000.0, -exponents).astype(np.float32)
    freq = jnp.asarray(np.concatenate([freq, freq])[None, :])
    vmem = pl.BlockSpec(memory_space=pltpu.VMEM)
    dma = pltpu.SemaphoreType.DMA
    kv, wg, gg = pl.pallas_call(
        functools.partial(kernel, ny, nz),
        out_shape=(
            jax.ShapeDtypeStruct((rows, cols), BF16),
            jax.ShapeDtypeStruct((shard, cols), F32),
            jax.ShapeDtypeStruct((1, shard), F32),
        ),
        in_specs=[vmem] * 8,
        out_specs=(vmem, vmem, vmem),
        scratch_shapes=[
            pltpu.VMEM((shard, cols), BF16),
            pltpu.VMEM((jn, 2, shard, LANES), BF16),
            pltpu.VMEM((jn, slab, LANES), BF16),
            pltpu.VMEM((jn, 4, 2, slab, cols), BF16),
            pltpu.VMEM((jn, 4, 2, slab, cols), BF16),
            pltpu.VMEM((jn, 4, slab, cols), BF16),
            pltpu.VMEM((jn, 4, slab, cols), BF16),
            pltpu.VMEM((plane, jn, slab, LANES), BF16),
            pltpu.VMEM((jn, 2, shard, LANES), BF16),
            pltpu.VMEM((steps, shard, LANES), BF16),
            pltpu.VMEM((shard, LANES), F32),
            pltpu.VMEM((4, shard, cols), F32),
            pltpu.VMEM((rows, cols), BF16),
            dma((steps,)),
            dma((jn, 2)),
            dma((plane,)),
            dma((plane,)),
            dma,
            dma,
            dma,
            dma,
            dma((plane,)),
            dma((plane,)),
            dma((steps,)),
            dma((steps,)),
            dma((plane,)),
            dma((plane,)),
        ],
        compiler_params=pltpu.CompilerParams(
            collective_id=0, has_side_effects=True, vmem_limit_bytes=40 * 2**20
        ),
        name="kv_exchange",
    )(
        counts,
        ratios.reshape(1, -1),
        gain.reshape(1, -1),
        kv_weight,
        positions.reshape(-1, LANES),
        freq,
        tokens,
        cotangent,
    )
    return (kv, wg, gg.reshape(-1))


def solution(mesh):
    ny = mesh.shape["dom"] // 4
    nz = mesh.shape["fsdp"] // 2
    return jax.shard_map(
        functools.partial(body, ny, nz),
        mesh=mesh,
        in_specs=(
            P(("dom", "fsdp"), None),
            P("fsdp"),
            P("fsdp", None),
            P(("dom", "fsdp")),
            P(("dom", "fsdp"), None),
            P(),
            P(),
        ),
        out_specs=(P(("dom", "fsdp"), None), P("fsdp", None), P("fsdp")),
        check_vma=False,
    )
```

```python
import functools

import jax
import jax.numpy as jnp
import numpy as np
from jax import lax
from jax.experimental import pallas as pl
from jax.experimental.pallas import tpu as pltpu
from jax.sharding import PartitionSpec as P

HD = 128
HALF = HD // 2
BLOCK = 128
LANES = 128
MESH = pl.DeviceIdType.MESH
F32 = jnp.float32
BF16 = jnp.bfloat16


def to_column(row, size):
    eye = lax.broadcasted_iota(jnp.int32, (size, size), 0) == lax.broadcasted_iota(
        jnp.int32, (size, size), 1
    )
    return jnp.sum(jnp.where(eye, row, jnp.float32(0.0)), axis=1, keepdims=True)


def to_row(column, size):
    eye = lax.broadcasted_iota(jnp.int32, (size, size), 0) == lax.broadcasted_iota(
        jnp.int32, (size, size), 1
    )
    return jnp.sum(jnp.where(eye, column, jnp.float32(0.0)), axis=0, keepdims=True)


def kernel(
    ny,
    nz,
    counts_hbm,
    ratios_hbm,
    gain_hbm,
    weight_hbm,
    positions_hbm,
    freq_hbm,
    tokens_hbm,
    cot_hbm,
    kv_ref,
    wg_ref,
    gg_ref,
    counts_ref,
    ratios_ref,
    gain_ref,
    weight_ref,
    positions_ref,
    freq_ref,
    tokens_ref,
    cot_ref,
    own_gw,
    land_g1,
    piece_g,
    full_gw,
    part_m,
    land_r0,
    sum_r0,
    land_r1,
    sum_r1,
    land_r2,
    sum_r2,
    land_r3,
    upstream,
    sem_in,
    sem_g1s,
    sem_g1r,
    sem_gxs,
    sem_gxr,
    sem_g2s,
    sem_g2r,
    sem_g3s,
    sem_g3r,
    sem_r0s,
    sem_r0r,
    sem_r1s,
    sem_r1r,
    sem_r2s,
    sem_r2r,
    sem_r3s,
    sem_r3r,
):
    dom = lax.axis_index("dom")
    fsdp = lax.axis_index("fsdp")
    core = lax.rem(dom, 2)
    y = lax.rem(dom // 2, ny)
    x_hi = dom // (2 * ny)
    z = fsdp // 2
    x_lo = lax.rem(fsdp, 2)
    x = x_hi * 2 + x_lo
    q = x_hi * 2 + core
    jn = nz // 8
    plane = 4 * ny
    steps = 2 * jn
    rows, width = tokens_ref.shape
    shard, cols = weight_ref.shape
    slab = 2 * shard
    key_width = cols // 2
    heads = key_width // HD
    group = 8 * slab
    lo_own = lax.rem(z + core, 2)
    lo_sib = 1 - lo_own

    def dev(xx, yy, cc, zz):
        return ((xx // 2 * ny + yy) * 2 + cc, zz * 2 + lax.rem(xx, 2))

    def remote(src, dst, send, recv, device):
        return pltpu.make_async_remote_copy(
            src_ref=src,
            dst_ref=dst,
            send_sem=send,
            recv_sem=recv,
            device_id=device,
            device_id_type=MESH,
        )

    def lane_tile(i):
        return pl.ds(pl.multiple_of(i * LANES, LANES), LANES)

    def wrap_z(value):
        return lax.rem(value + 2 * nz, nz)

    loads = [
        pltpu.make_async_copy(src, dst, sem_in.at[i])
        for i, (src, dst) in enumerate(
            (
                (tokens_hbm, tokens_ref),
                (cot_hbm, cot_ref),
                (positions_hbm, positions_ref),
                (freq_hbm, freq_ref),
                (weight_hbm, weight_ref),
                (gain_hbm, gain_ref),
                (counts_hbm, counts_ref),
                (ratios_hbm, ratios_ref),
            )
        )
    ]
    for load in loads:
        load.start()

    own_class = q + 4 * x_lo
    own_shift = q - 4 * x_lo
    residue = lax.rem(z - own_class + 2 * nz, 8)
    hi_own = residue // 2
    home = wrap_z(z - own_shift) // 8

    barrier = pltpu.get_barrier_semaphore()

    def greet(device):
        pl.semaphore_signal(barrier, inc=1, device_id=device, device_id_type=MESH)

    def greet_plane(i, carry):
        xx = lax.rem(x + i // (2 * ny), 4)
        yy = lax.rem(y + lax.rem(i // 2, ny), ny)
        cc = lax.rem(core + lax.rem(i, 2), 2)
        greet(dev(xx, yy, cc, z))
        return carry

    lax.fori_loop(1, 2 * plane, greet_plane, 0)
    near_self = (own_class == 0).astype(jnp.int32)
    for half in range(2):
        owner = dev(x_hi * 2 + half, y, core, wrap_z(z - own_shift))
        if half == 0:

            @pl.when(own_class != 0)
            def _(owner=owner):
                greet(owner)

        else:
            greet(owner)
    ring = min(jn - 1, 2)
    ahead = dev(x, y, core, wrap_z(z + 8))
    behind = dev(x, y, core, wrap_z(z - 8))
    if jn > 1:
        greet(ahead)
    if jn > 2:
        greet(behind)

    loads[4].wait()
    loads[5].wait()
    gain_col = to_column(gain_ref[...].astype(F32), shard)
    weight = weight_ref[...].astype(F32)
    own_gw[...] = (weight * gain_col).astype(BF16)

    loads[2].wait()
    loads[3].wait()
    pos = positions_ref[...].astype(F32)
    pos_col = jnp.concatenate(
        [to_column(pos[i : i + 1, :], LANES) for i in range(rows // LANES)], axis=0
    )
    angles = pos_col * freq_ref[...]
    cosines = jnp.cos(angles)
    lane_ids = lax.broadcasted_iota(jnp.int32, (rows, HD), 1)
    sines = jnp.where(lane_ids < HALF, -1.0, 1.0) * jnp.sin(angles)

    loads[6].wait()
    loads[7].wait()
    counts = counts_ref[...].astype(F32)
    n_dom, n_mem = counts.shape
    domain_rows = BLOCK * jnp.sum(counts, axis=1, keepdims=True)
    live_total = jnp.sum(domain_rows, axis=0, keepdims=True)
    ratio = to_column(ratios_ref[...].astype(F32), n_dom)
    factor = ratio / jnp.sum(ratio, axis=0, keepdims=True) * live_total / domain_rows
    dom_ids = lax.broadcasted_iota(jnp.int32, (n_dom, 1), 0)
    own_factor = jnp.sum(jnp.where(dom_ids == dom, factor, 0.0), axis=0, keepdims=True)
    at_dom = lax.broadcasted_iota(jnp.int32, (n_dom, n_mem), 0) == dom
    at_mem = lax.broadcasted_iota(jnp.int32, (n_dom, n_mem), 1) == fsdp
    own_count = jnp.sum(
        jnp.sum(jnp.where(at_dom & at_mem, counts, 0.0), axis=1, keepdims=True),
        axis=0,
        keepdims=True,
    )
    row_ids = lax.broadcasted_iota(jnp.int32, (rows, 1), 0).astype(F32)
    row_factor = jnp.where(row_ids < BLOCK * own_count, own_factor, 0.0)

    loads[0].wait()
    token = tokens_ref[...].astype(F32)
    mean_square = jnp.sum(token * token, axis=1, keepdims=True) * (1.0 / width)
    inv_norm = lax.rsqrt(mean_square + 1e-06)

    loads[1].wait()
    scale = row_factor * inv_norm
    for h in range(2 * heads):
        part = cot_ref[:, h * HD : (h + 1) * HD].astype(F32) * scale
        if h < heads:
            part = part * cosines - pltpu.roll(part, HALF, 1) * sines
        upstream[:, h * HD : (h + 1) * HD] = part.astype(BF16)

    pl.semaphore_wait(barrier, 2 * plane - 1 + 2 + ring - near_self)

    def g1_copy(t):
        return remote(
            own_gw.at[:, lane_tile(y)],
            land_g1.at[x_lo],
            sem_g1s.at[t],
            sem_g1r.at[x_lo],
            dev(x_hi * 2 + t, y, core, wrap_z(z + q - 4 * t)),
        )

    g1_local = pltpu.make_async_copy(
        own_gw.at[:, lane_tile(y)], land_g1.at[0], sem_g1r.at[0]
    )

    @pl.when(own_class != 0)
    def _():
        g1_copy(0).start()

    @pl.when(own_class == 0)
    def _():
        g1_local.start()

    g1_copy(1).start()

    sibling = dev(x, y, 1 - core, z)

    def r0_copy(j):
        return remote(
            part_m.at[j, :, lo_sib],
            land_r0.at[j],
            sem_r0s.at[j],
            sem_r0r.at[j],
            sibling,
        )

    def m_step(j, carry):
        lhs = tokens_ref[:, pl.ds(pl.multiple_of(j * group, group), group)]
        prod = lax.dot_general(
            lhs, upstream[...], (((0,), (0,)), ((), ())), preferred_element_type=F32
        )
        part_m[j] = prod.reshape(4, 2, slab, cols).astype(BF16)
        r0_copy(j).start()
        return carry

    lax.fori_loop(0, jn, m_step, 0)

    def neighbour(k):
        return lax.rem(x + k // ny, 4), lax.rem(y + lax.rem(k, ny), ny)

    def r1_copy(k, j):
        xx, yy = neighbour(k)
        to_class = (xx // 2) * 2 + core + 4 * lax.rem(xx, 2)
        hi = lax.rem(z - to_class + 2 * nz, 8) // 2
        return remote(
            sum_r0.at[j, hi, :, lane_tile(yy)],
            land_r1.at[k, j],
            sem_r1s.at[k, j],
            sem_r1r.at[k, j],
            dev(xx, yy, core, z),
        )

    def r1_send(j, carry):
        r0_copy(j).wait_recv()
        total = part_m[j, :, lo_own].astype(F32) + land_r0[j].astype(F32)
        sum_r0[j] = total.astype(BF16)

        def one(k, c):
            r1_copy(k, j).start()
            return c

        return lax.fori_loop(1, plane, one, carry)

    lax.fori_loop(0, jn, r1_send, 0)

    for half in range(2):
        pltpu.make_async_copy(
            land_g1.at[half], land_g1.at[half], sem_g1r.at[half]
        ).wait()
    piece_g[home] = jnp.concatenate(
        [land_g1[0].astype(F32), land_g1[1].astype(F32)], axis=0
    ).astype(BF16)

    def ring_copy(i, at, device):
        return remote(
            piece_g.at[at], piece_g.at[at], sem_gxs.at[i], sem_gxr.at[i], device
        )

    def nth(i):
        return lax.rem(home + i + 2 * jn, jn)

    if jn > 1:
        ring_copy(0, home, ahead).start()
    if jn > 2:
        ring_copy(1, home, behind).start()

    def r1_arrive(j, carry):
        def one(k, total):
            r1_copy(k, j).wait_recv()
            return total + land_r1[k, j].astype(F32)

        total = lax.fori_loop(
            1, plane, one, sum_r0[j, hi_own, :, lane_tile(y)].astype(F32)
        )
        for half in range(2):
            sum_r1[j, half] = total[half * shard : (half + 1) * shard, :].astype(BF16)
        return carry

    lax.fori_loop(0, jn // 2, r1_arrive, 0)
    if jn > 1:
        ring_copy(0, nth(-1), behind).wait_recv()
    if jn > 3:
        ring_copy(2, nth(-1), ahead).start()
    lax.fori_loop(jn // 2, jn, r1_arrive, 0)
    if jn > 2:
        ring_copy(1, nth(1), ahead).wait_recv()
    if jn > 3:
        ring_copy(2, nth(2), behind).wait_recv()

    def r2_copy(i):
        a, half = i // 2, lax.rem(i, 2)
        far = 8 * a + residue
        slot = 2 * (wrap_z(z - own_class - far) // 8) + x_lo
        return (
            (far == z) & (half == x_lo),
            remote(
                sum_r1.at[a, half],
                land_r2.at[slot],
                sem_r2s.at[i],
                sem_r2r.at[slot],
                dev(x_hi * 2 + half, y, core, far),
            ),
        )

    r2_local = pltpu.make_async_copy(
        sum_r1.at[z // 8, x_lo], land_r2.at[0], sem_r2r.at[0]
    )

    def r2_start(i, carry):
        stays, copy = r2_copy(i)

        @pl.when(jnp.logical_not(stays))
        def _():
            copy.start()

        @pl.when(stays)
        def _():
            r2_local.start()

        return carry

    lax.fori_loop(0, steps, r2_start, 0)

    def g2_copy(k):
        xx, yy = neighbour(k)
        return remote(
            piece_g,
            full_gw.at[:, hi_own, lo_own, :, lane_tile(y)],
            sem_g2s.at[k],
            sem_g2r.at[k],
            dev(xx, yy, core, z),
        )

    g2_local = pltpu.make_async_copy(
        piece_g, full_gw.at[:, hi_own, lo_own, :, lane_tile(y)], sem_g2r.at[0]
    )
    g2_local.start()

    def g2_start(k, carry):
        g2_copy(k).start()
        return carry

    lax.fori_loop(1, plane, g2_start, 0)

    def g3_copy(k, lo):
        xx = lax.rem(x - k // ny + 4, 4)
        yy = lax.rem(y - lax.rem(k, ny) + ny, ny)
        from_class = (xx // 2) * 2 + 4 * lax.rem(xx, 2) + lax.rem(core + lo_own + lo, 2)
        hi = lax.rem(z - from_class + 2 * nz, 8) // 2
        view = full_gw.at[:, hi, lo, :, lane_tile(yy)]
        return remote(view, view, sem_g3s.at[k], sem_g3r.at[k], sibling)

    g2_local.wait()
    g3_copy(0, lo_own).start()

    def g2_arrive(k, carry):
        g2_copy(k).wait_recv()
        g3_copy(k, lo_own).start()
        return carry

    lax.fori_loop(1, plane, g2_arrive, 0)

    def r2_arrive(s, total):
        pltpu.make_async_copy(land_r2.at[s], land_r2.at[s], sem_r2r.at[s]).wait()
        return total + land_r2[s].astype(F32)

    sum_r2[...] = lax.fori_loop(0, steps, r2_arrive, jnp.zeros((shard, LANES), F32))

    def r3_copy(i):
        hh = lax.rem(x_hi + i // (2 * ny), 2)
        yy = lax.rem(y + lax.rem(i // 2, ny), ny)
        cc = lax.rem(core + lax.rem(i, 2), 2)
        return remote(
            sum_r2,
            land_r3.at[q, :, lane_tile(y)],
            sem_r3s.at[i],
            sem_r3r.at[i],
            dev(hh * 2 + x_lo, yy, cc, z),
        )

    r3_local = pltpu.make_async_copy(
        sum_r2, land_r3.at[q, :, lane_tile(y)], sem_r3r.at[0]
    )
    r3_local.start()

    def r3_start(i, carry):
        r3_copy(i).start()
        return carry

    lax.fori_loop(1, plane, r3_start, 0)

    def g3_arrive(k, carry):
        g3_copy(k, lo_sib).wait_recv()
        return carry

    lax.fori_loop(0, plane, g3_arrive, 0)

    def p_step(j, total):
        lhs = tokens_ref[:, pl.ds(pl.multiple_of(j * group, group), group)]
        rhs = full_gw[j].reshape(group, cols)
        return total + jnp.dot(lhs, rhs, preferred_element_type=F32)

    projected = lax.fori_loop(0, jn, p_step, jnp.zeros((rows, cols), F32))
    projected = projected * inv_norm
    for h in range(2 * heads):
        part = projected[:, h * HD : (h + 1) * HD]
        if h < heads:
            part = part * cosines + pltpu.roll(part, HALF, 1) * sines
        kv_ref[:, h * HD : (h + 1) * HD] = part.astype(BF16)

    r3_local.wait()

    def r3_arrive(i, carry):
        r3_copy(i).wait_recv()
        return carry

    lax.fori_loop(1, plane, r3_arrive, 0)
    total = land_r3[0] + land_r3[1] + land_r3[2] + land_r3[3]
    root = jnp.sqrt(live_total)
    wg_ref[...] = total * gain_col / root
    gain_sum = jnp.sum(total * weight, axis=1, keepdims=True)
    gg_ref[...] = to_row(gain_sum / root, shard)

    @pl.when(own_class != 0)
    def _():
        g1_copy(0).wait_send()

    g1_copy(1).wait_send()
    for i in range(min(jn - 1, 3)):
        ring_copy(i, home, ahead).wait_send()

    def r2_drain(i, carry):
        stays, copy = r2_copy(i)

        @pl.when(jnp.logical_not(stays))
        def _():
            copy.wait_send()

        return carry

    def r0_drain(j, carry):
        r0_copy(j).wait_send()
        return carry

    def drain(k, carry):
        g2_copy(k).wait_send()
        r3_copy(k).wait_send()

        def one(j, c):
            r1_copy(k, j).wait_send()
            return c

        return lax.fori_loop(0, jn, one, carry)

    def g3_drain(k, carry):
        g3_copy(k, lo_own).wait_send()
        return carry

    lax.fori_loop(0, steps, r2_drain, 0)
    lax.fori_loop(0, jn, r0_drain, 0)
    lax.fori_loop(1, plane, drain, 0)
    lax.fori_loop(0, plane, g3_drain, 0)


def body(ny, nz, tokens, gain, kv_weight, positions, cotangent, counts, ratios):
    rows, width = tokens.shape
    shard, cols = kv_weight.shape
    jn, plane = nz // 8, 4 * ny
    steps = 2 * jn
    slab = 2 * shard
    exponents = np.arange(HALF) * (2.0 / HD)
    freq = np.power(1000000.0, -exponents).astype(np.float32)
    freq = jnp.asarray(np.concatenate([freq, freq])[None, :])
    operands = (
        counts,
        ratios.reshape(1, -1),
        gain.reshape(1, -1),
        kv_weight,
        positions.reshape(-1, LANES),
        freq,
        tokens,
        cotangent,
    )
    vmem = pl.BlockSpec(memory_space=pltpu.VMEM)
    dma = pltpu.SemaphoreType.DMA
    kv, wg, gg = pl.pallas_call(
        functools.partial(kernel, ny, nz),
        out_shape=(
            jax.ShapeDtypeStruct((rows, cols), BF16),
            jax.ShapeDtypeStruct((shard, cols), F32),
            jax.ShapeDtypeStruct((1, shard), F32),
        ),
        in_specs=[pl.BlockSpec(memory_space=pltpu.HBM)] * len(operands),
        out_specs=(vmem, vmem, vmem),
        scratch_shapes=[pltpu.VMEM(v.shape, v.dtype) for v in operands]
        + [
            pltpu.VMEM((shard, cols), BF16),
            pltpu.VMEM((2, shard, LANES), BF16),
            pltpu.VMEM((jn, slab, LANES), BF16),
            pltpu.VMEM((jn, 4, 2, slab, cols), BF16),
            pltpu.VMEM((jn, 4, 2, slab, cols), BF16),
            pltpu.VMEM((jn, 4, slab, cols), BF16),
            pltpu.VMEM((jn, 4, slab, cols), BF16),
            pltpu.VMEM((plane, jn, slab, LANES), BF16),
            pltpu.VMEM((jn, 2, shard, LANES), BF16),
            pltpu.VMEM((steps, shard, LANES), BF16),
            pltpu.VMEM((shard, LANES), F32),
            pltpu.VMEM((4, shard, cols), F32),
            pltpu.VMEM((rows, cols), BF16),
            dma((len(operands),)),
            dma((2,)),
            dma((2,)),
            dma((3,)),
            dma((3,)),
            dma((plane,)),
            dma((plane,)),
            dma((plane,)),
            dma((plane,)),
            dma((jn,)),
            dma((jn,)),
            dma((plane, jn)),
            dma((plane, jn)),
            dma((steps,)),
            dma((steps,)),
            dma((plane,)),
            dma((plane,)),
        ],
        compiler_params=pltpu.CompilerParams(
            collective_id=0, has_side_effects=True, vmem_limit_bytes=56 * 2**20
        ),
        name="kv_exchange",
    )(*operands)
    return (kv, wg, gg.reshape(-1))


def solution(mesh):
    ny = mesh.shape["dom"] // 4
    nz = mesh.shape["fsdp"] // 2
    return jax.shard_map(
        functools.partial(body, ny, nz),
        mesh=mesh,
        in_specs=(
            P(("dom", "fsdp"), None),
            P("fsdp"),
            P("fsdp", None),
            P(("dom", "fsdp")),
            P(("dom", "fsdp"), None),
            P(),
            P(),
        ),
        out_specs=(P(("dom", "fsdp"), None), P("fsdp", None), P("fsdp")),
        check_vma=False,
    )
```

```python
import functools

import jax
import jax.numpy as jnp
import numpy as np
from jax import lax
from jax.experimental import pallas as pl
from jax.experimental.pallas import tpu as pltpu
from jax.sharding import PartitionSpec as P

HD = 128
HALF = HD // 2
BLOCK = 128
LANES = 128
MESH = pl.DeviceIdType.MESH
F32 = jnp.float32
BF16 = jnp.bfloat16


def to_column(row, size):
    eye = lax.broadcasted_iota(jnp.int32, (size, size), 0) == lax.broadcasted_iota(
        jnp.int32, (size, size), 1
    )
    return jnp.sum(jnp.where(eye, row, jnp.float32(0.0)), axis=1, keepdims=True)


def to_row(column, size):
    eye = lax.broadcasted_iota(jnp.int32, (size, size), 0) == lax.broadcasted_iota(
        jnp.int32, (size, size), 1
    )
    return jnp.sum(jnp.where(eye, column, jnp.float32(0.0)), axis=0, keepdims=True)


def kernel(
    ny,
    nz,
    counts_hbm,
    ratios_hbm,
    gain_hbm,
    weight_hbm,
    positions_hbm,
    freq_hbm,
    tokens_hbm,
    cot_hbm,
    kv_hbm,
    wg_hbm,
    gg_hbm,
    counts_ref,
    ratios_ref,
    gain_ref,
    weight_ref,
    positions_ref,
    freq_ref,
    tokens_ref,
    cot_ref,
    own_gw,
    land_g1,
    piece_g,
    full_gw,
    part_m,
    land_r0,
    sum_r0,
    land_r1,
    sum_r1,
    land_r2,
    sum_r2,
    land_r3,
    upstream,
    kv_ref,
    wg_ref,
    gg_ref,
    sem_in,
    sem_out,
    sem_g1s,
    sem_g1r,
    sem_gxs,
    sem_gxr,
    sem_g2s,
    sem_g2r,
    sem_g3s,
    sem_g3r,
    sem_r0s,
    sem_r0r,
    sem_r1s,
    sem_r1r,
    sem_r2s,
    sem_r2r,
    sem_r3s,
    sem_r3r,
):
    dom = lax.axis_index("dom")
    fsdp = lax.axis_index("fsdp")
    core = lax.rem(dom, 2)
    y = lax.rem(lax.div(dom, 2), ny)
    x_hi = lax.div(dom, 2 * ny)
    z = lax.div(fsdp, 2)
    x_lo = lax.rem(fsdp, 2)
    x = x_hi * 2 + x_lo
    q = x_hi * 2 + core
    jn = nz // 8
    plane = 4 * ny
    steps = 2 * jn
    rows, width = tokens_ref.shape
    shard, cols = weight_ref.shape
    slab = 2 * shard
    key_width = cols // 2
    heads = key_width // HD
    group = 8 * slab
    lo_own = lax.rem(z + core, 2)
    lo_sib = 1 - lo_own

    def dev(xx, yy, cc, zz):
        return (lax.div(xx, 2) * (2 * ny) + yy * 2 + cc, zz * 2 + lax.rem(xx, 2))

    def remote(src, dst, send, recv, device):
        return pltpu.make_async_remote_copy(
            src_ref=src,
            dst_ref=dst,
            send_sem=send,
            recv_sem=recv,
            device_id=device,
            device_id_type=MESH,
        )

    def lane_tile(i):
        return pl.ds(pl.multiple_of(i * LANES, LANES), LANES)

    def wrap_z(value):
        return lax.rem(value + 2 * nz, nz)

    loads = [
        pltpu.make_async_copy(src, dst, sem_in.at[i])
        for i, (src, dst) in enumerate(
            (
                (tokens_hbm, tokens_ref),
                (cot_hbm, cot_ref),
                (positions_hbm, positions_ref),
                (freq_hbm, freq_ref),
                (weight_hbm, weight_ref),
                (gain_hbm, gain_ref),
                (counts_hbm, counts_ref),
                (ratios_hbm, ratios_ref),
            )
        )
    ]
    for load in loads:
        load.start()

    own_class = q + 4 * x_lo
    own_shift = q - 4 * x_lo
    residue = lax.rem(z - own_class + 2 * nz, 8)
    hi_own = lax.div(residue, 2)
    home = lax.div(wrap_z(z - own_shift), 8)

    barrier = pltpu.get_barrier_semaphore()

    def greet(device):
        pl.semaphore_signal(barrier, inc=1, device_id=device, device_id_type=MESH)

    xs = [lax.rem(x + i, 4) for i in range(4)]
    ys = [lax.rem(y + i, ny) for i in range(ny)]

    def class_of(xx, cc):
        return lax.div(xx, 2) * 2 + cc + 4 * lax.rem(xx, 2)

    def hi_of(xx, cc):
        return lax.div(lax.rem(z - class_of(xx, cc) + 2 * nz, 8), 2)

    his = [hi_of(xx, core) for xx in xs]
    at_plane = [[dev(xx, yy, core, z) for yy in ys] for xx in xs]
    at_other = [[(a + 1 - 2 * core, b) for a, b in line] for line in at_plane]
    sibling = at_other[0][0]
    peers = [(i, j) for i in range(4) for j in range(ny)][1:]

    greet(sibling)
    for i, j in peers:
        greet(at_plane[i][j])
        greet(at_other[i][j])
    near_self = (own_class == 0).astype(jnp.int32)
    for half in range(2):
        owner = dev(x_hi * 2 + half, y, core, wrap_z(z - own_shift))
        if half == 0:

            @pl.when(own_class != 0)
            def _(owner=owner):
                greet(owner)

        else:
            greet(owner)
    ring = min(jn - 1, 2)
    ahead = dev(x, y, core, wrap_z(z + 8))
    behind = dev(x, y, core, wrap_z(z - 8))
    if jn > 1:
        greet(ahead)
    if jn > 2:
        greet(behind)

    loads[4].wait()
    loads[5].wait()
    gain_col = to_column(gain_ref[...].astype(F32), shard)
    weight = weight_ref[...].astype(F32)
    own_gw[...] = (weight * gain_col).astype(BF16)

    loads[2].wait()
    loads[3].wait()
    pos = positions_ref[...].astype(F32)
    pos_col = jnp.concatenate(
        [to_column(pos[i : i + 1, :], LANES) for i in range(rows // LANES)], axis=0
    )
    angles = pos_col * freq_ref[...]
    cosines = jnp.cos(angles)
    lane_ids = lax.broadcasted_iota(jnp.int32, (rows, HD), 1)
    sines = jnp.where(lane_ids < HALF, -1.0, 1.0) * jnp.sin(angles)

    loads[6].wait()
    loads[7].wait()
    counts = counts_ref[...].astype(F32)
    n_dom, n_mem = counts.shape
    domain_rows = BLOCK * jnp.sum(counts, axis=1, keepdims=True)
    live_total = jnp.sum(domain_rows, axis=0, keepdims=True)
    ratio = to_column(ratios_ref[...].astype(F32), n_dom)
    factor = ratio / jnp.sum(ratio, axis=0, keepdims=True) * live_total / domain_rows
    dom_ids = lax.broadcasted_iota(jnp.int32, (n_dom, 1), 0)
    own_factor = jnp.sum(jnp.where(dom_ids == dom, factor, 0.0), axis=0, keepdims=True)
    at_dom = lax.broadcasted_iota(jnp.int32, (n_dom, n_mem), 0) == dom
    at_mem = lax.broadcasted_iota(jnp.int32, (n_dom, n_mem), 1) == fsdp
    own_count = jnp.sum(
        jnp.sum(jnp.where(at_dom & at_mem, counts, 0.0), axis=1, keepdims=True),
        axis=0,
        keepdims=True,
    )
    row_ids = lax.broadcasted_iota(jnp.int32, (rows, 1), 0).astype(F32)
    row_factor = jnp.where(row_ids < BLOCK * own_count, own_factor, 0.0)

    loads[0].wait()
    token = tokens_ref[...].astype(F32)
    mean_square = jnp.sum(token * token, axis=1, keepdims=True) * (1.0 / width)
    inv_norm = lax.rsqrt(mean_square + 1e-06)

    loads[1].wait()
    scale = row_factor * inv_norm
    for h in range(2 * heads):
        part = cot_ref[:, h * HD : (h + 1) * HD].astype(F32) * scale
        if h < heads:
            part = part * cosines - pltpu.roll(part, HALF, 1) * sines
        upstream[:, h * HD : (h + 1) * HD] = part.astype(BF16)

    pl.semaphore_wait(barrier, 2 * plane - 1 + 2 + ring - near_self)

    def g1_copy(t):
        return remote(
            own_gw.at[:, lane_tile(y)],
            land_g1.at[x_lo],
            sem_g1s.at[t],
            sem_g1r.at[x_lo],
            dev(x_hi * 2 + t, y, core, wrap_z(z + q - 4 * t)),
        )

    g1_local = pltpu.make_async_copy(
        own_gw.at[:, lane_tile(y)], land_g1.at[0], sem_g1r.at[0]
    )

    @pl.when(own_class != 0)
    def _():
        g1_copy(0).start()

    @pl.when(own_class == 0)
    def _():
        g1_local.start()

    g1_copy(1).start()

    def r0_copy(j):
        return remote(
            part_m.at[j, :, lo_sib], land_r0.at[j], sem_r0s, sem_r0r.at[j], sibling
        )

    def m_step(j, carry):
        lhs = tokens_ref[:, pl.ds(pl.multiple_of(j * group, group), group)]
        prod = lax.dot_general(
            lhs, upstream[...], (((0,), (0,)), ((), ())), preferred_element_type=F32
        )
        part_m[j] = prod.reshape(4, 2, slab, cols).astype(BF16)
        r0_copy(j).start()
        return carry

    lax.fori_loop(0, jn, m_step, 0)

    def r1_send(j, carry):
        r0_copy(j).wait_recv()
        total = part_m[j, :, lo_own].astype(F32) + land_r0[j].astype(F32)
        sum_r0[j] = total.astype(BF16)
        for k, (dx, dy) in enumerate(peers):
            remote(
                sum_r0.at[j, his[dx], :, lane_tile(ys[dy])],
                land_r1.at[j, k],
                sem_r1s,
                sem_r1r.at[j],
                at_plane[dx][dy],
            ).start()
        return carry

    lax.fori_loop(0, jn, r1_send, 0)

    for half in range(2):
        pltpu.make_async_copy(
            land_g1.at[half], land_g1.at[half], sem_g1r.at[half]
        ).wait()
    piece_g[home] = jnp.concatenate(
        [land_g1[0].astype(F32), land_g1[1].astype(F32)], axis=0
    ).astype(BF16)

    def ring_copy(i, at, device):
        return remote(
            piece_g.at[at], piece_g.at[at], sem_gxs.at[i], sem_gxr.at[i], device
        )

    def nth(i):
        return lax.rem(home + i + 2 * jn, jn)

    if jn > 1:
        ring_copy(0, home, ahead).start()
    if jn > 2:
        ring_copy(1, home, behind).start()

    def arrived(buffer, sem):
        pltpu.make_async_copy(buffer, buffer, sem).wait()

    def r1_arrive(j, carry):
        arrived(land_r1.at[j], sem_r1r.at[j])

        total = sum_r0[j, hi_own, :, lane_tile(y)].astype(F32)
        for k in range(plane - 1):
            total = total + land_r1[j, k].astype(F32)
        for half in range(2):
            sum_r1[j, half] = total[half * shard : (half + 1) * shard, :].astype(BF16)
        return carry

    lax.fori_loop(0, 1, r1_arrive, 0)
    if jn > 1:
        ring_copy(0, nth(-1), behind).wait_recv()
    if jn > 3:
        ring_copy(2, nth(-1), ahead).start()
    lax.fori_loop(1, jn, r1_arrive, 0)
    if jn > 2:
        ring_copy(1, nth(1), ahead).wait_recv()
    if jn > 3:
        ring_copy(2, nth(2), behind).wait_recv()

    order = sorted(range(jn), key=lambda i: -min(i, jn - i))

    def r2_copy(i, half):
        far = wrap_z(z - own_shift + 8 * i)
        slot = 2 * lax.div(wrap_z(z - own_class - far), 8) + x_lo
        return remote(
            sum_r1.at[nth(i), half],
            land_r2.at[slot],
            sem_r2s,
            sem_r2r,
            dev(x_hi * 2 + half, y, core, far),
        )

    r2_local = pltpu.make_async_copy(
        sum_r1.at[home, 0], land_r2.at[0], sem_r2r
    )
    for i in order:
        for half in range(2):
            if i == 0 and half == 0:

                @pl.when(own_class != 0)
                def _():
                    r2_copy(0, 0).start()

                @pl.when(own_class == 0)
                def _():
                    r2_local.start()

            else:
                r2_copy(i, half).start()

    g2_view = full_gw.at[:, hi_own, lo_own, :, lane_tile(y)]
    pltpu.make_async_copy(piece_g, g2_view, sem_g2r.at[0]).start()
    for dx, dy in peers:
        remote(piece_g, g2_view, sem_g2s, sem_g2r.at[dx], at_plane[dx][dy]).start()

    arrived(land_r0, sem_r0s)
    arrived(land_r1, sem_r1s)

    @pl.when(own_class != 0)
    def _():
        g1_copy(0).wait_send()

    g1_copy(1).wait_send()
    for i in range(min(jn - 1, 3)):
        ring_copy(i, home, ahead).wait_send()

    def g3_copy(hi, lo, i):
        view = full_gw.at[:, hi, lo]
        return remote(view, view, sem_g3s, sem_g3r.at[i], sibling)

    for dx in range(4):
        back = (4 - dx) % 4
        arrived(full_gw.at[:, his[back], lo_own], sem_g2r.at[dx])
        g3_copy(his[back], lo_own, dx).start()

    arrived(land_r2, sem_r2r)
    total2 = land_r2[0].astype(F32)
    for s in range(1, steps):
        total2 = total2 + land_r2[s].astype(F32)
    sum_r2[...] = total2

    slot3 = 4 * y + q
    pltpu.make_async_copy(sum_r2, land_r3.at[slot3], sem_r3r).start()

    def r3_send(device):
        remote(sum_r2, land_r3.at[slot3], sem_r3s, sem_r3r, device).start()

    r3_send(sibling)
    for dx in (0, 2):
        for dy in range(ny):
            if dx or dy:
                r3_send(at_plane[dx][dy])
                r3_send(at_other[dx][dy])

    for dx in range(4):
        back = (4 - dx) % 4
        arrived(full_gw.at[:, hi_of(xs[back], 1 - core), lo_sib], sem_g3r.at[dx])

    def p_step(j, total):
        lhs = tokens_ref[:, pl.ds(pl.multiple_of(j * group, group), group)]
        rhs = full_gw[j].reshape(group, cols)
        return total + jnp.dot(lhs, rhs, preferred_element_type=F32)

    projected = lax.fori_loop(0, jn, p_step, jnp.zeros((rows, cols), F32))
    projected = projected * inv_norm
    for h in range(2 * heads):
        part = projected[:, h * HD : (h + 1) * HD]
        if h < heads:
            part = part * cosines + pltpu.roll(part, HALF, 1) * sines
        kv_ref[:, h * HD : (h + 1) * HD] = part.astype(BF16)
    kv_out = pltpu.make_async_copy(kv_ref, kv_hbm, sem_out.at[0])
    kv_out.start()

    arrived(land_r3, sem_r3r)
    root = jnp.sqrt(live_total)
    gain_sum = jnp.zeros((shard, 1), F32)
    for i in range(ny):
        tile = slice(i * LANES, (i + 1) * LANES)
        total3 = land_r3[4 * i] + land_r3[4 * i + 1] + land_r3[4 * i + 2] + land_r3[4 * i + 3]
        wg_ref[:, tile] = total3 * gain_col / root
        gain_sum = gain_sum + jnp.sum(total3 * weight[:, tile], axis=1, keepdims=True)
    wg_out = pltpu.make_async_copy(wg_ref, wg_hbm, sem_out.at[1])
    wg_out.start()
    gg_ref[...] = to_row(gain_sum / root, shard)
    gg_out = pltpu.make_async_copy(gg_ref, gg_hbm, sem_out.at[2])
    gg_out.start()

    arrived(land_r1, sem_g2s)
    arrived(full_gw.at[:, :, lo_own], sem_g3s)

    @pl.when(own_class != 0)
    def _():
        arrived(land_r2, sem_r2s)

    @pl.when(own_class == 0)
    def _():
        arrived(land_r2.at[pl.ds(0, steps - 1)], sem_r2s)

    arrived(land_r3.at[pl.ds(0, plane - 1)], sem_r3s)
    kv_out.wait()
    wg_out.wait()
    gg_out.wait()


def copy_kernel(count, *refs):
    ins, outs, held = refs[:count], refs[count : 2 * count], refs[2 * count : 3 * count]
    sems = refs[-1]
    loads = [
        pltpu.make_async_copy(ins[i], held[i], sems.at[0, i]) for i in range(count)
    ]
    stores = [
        pltpu.make_async_copy(held[i], outs[i], sems.at[1, i]) for i in range(count)
    ]
    for load in loads:
        load.start()
    for load, store in zip(loads, stores):
        load.wait()
        store.start()
    for store in stores:
        store.wait()


def body(ny, nz, tokens, gain, kv_weight, positions, cotangent, counts, ratios):
    rows, width = tokens.shape
    shard, cols = kv_weight.shape
    jn, plane = nz // 8, 4 * ny
    steps = 2 * jn
    slab = 2 * shard
    exponents = np.arange(HALF) * (2.0 / HD)
    freq = np.power(1000000.0, -exponents).astype(np.float32)
    freq = jnp.asarray(np.concatenate([freq, freq])[None, :])
    operands = (
        counts,
        ratios.reshape(1, -1),
        gain.reshape(1, -1),
        kv_weight,
        positions.reshape(-1, LANES),
        freq,
        tokens,
        cotangent,
    )
    hbm = pl.BlockSpec(memory_space=pltpu.HBM)
    dma = pltpu.SemaphoreType.DMA
    shapes = (
        jax.ShapeDtypeStruct((rows, cols), BF16),
        jax.ShapeDtypeStruct((shard, cols), F32),
        jax.ShapeDtypeStruct((1, shard), F32),
    )
    outs = pl.pallas_call(
        functools.partial(kernel, ny, nz),
        out_shape=shapes,
        in_specs=[hbm] * len(operands),
        out_specs=(hbm, hbm, hbm),
        scratch_shapes=[pltpu.VMEM(v.shape, v.dtype) for v in operands]
        + [
            pltpu.VMEM((shard, cols), BF16),
            pltpu.VMEM((2, shard, LANES), BF16),
            pltpu.VMEM((jn, slab, LANES), BF16),
            pltpu.VMEM((jn, 4, 2, slab, cols), BF16),
            pltpu.VMEM((jn, 4, 2, slab, cols), BF16),
            pltpu.VMEM((jn, 4, slab, cols), BF16),
            pltpu.VMEM((jn, 4, slab, cols), BF16),
            pltpu.VMEM((jn, plane - 1, slab, LANES), BF16),
            pltpu.VMEM((jn, 2, shard, LANES), BF16),
            pltpu.VMEM((steps, shard, LANES), BF16),
            pltpu.VMEM((shard, LANES), F32),
            pltpu.VMEM((plane, shard, LANES), F32),
            pltpu.VMEM((rows, cols), BF16),
        ]
        + [pltpu.VMEM(v.shape, v.dtype) for v in shapes]
        + [
            dma((len(operands),)),
            dma((3,)),
            dma((2,)),
            dma((2,)),
            dma((3,)),
            dma((3,)),
            dma,
            dma((4,)),
            dma,
            dma((4,)),
            dma,
            dma((jn,)),
            dma,
            dma((jn,)),
            dma,
            dma,
            dma,
            dma,
        ],
        compiler_params=pltpu.CompilerParams(
            collective_id=0, has_side_effects=True, vmem_limit_bytes=56 * 2**20
        ),
        name="kv_exchange",
    )(*operands)
    kv, wg, gg = pl.pallas_call(
        functools.partial(copy_kernel, len(outs)),
        out_shape=shapes,
        in_specs=[hbm] * len(outs),
        out_specs=(hbm, hbm, hbm),
        scratch_shapes=[pltpu.VMEM(v.shape, v.dtype) for v in shapes]
        + [dma((2, len(outs)))],
        name="kv_outputs",
    )(*outs)
    return (kv, wg, gg.reshape(-1))


def solution(mesh):
    ny = mesh.shape["dom"] // 4
    nz = mesh.shape["fsdp"] // 2
    return jax.shard_map(
        functools.partial(body, ny, nz),
        mesh=mesh,
        in_specs=(
            P(("dom", "fsdp"), None),
            P("fsdp"),
            P("fsdp", None),
            P(("dom", "fsdp")),
            P(("dom", "fsdp"), None),
            P(),
            P(),
        ),
        out_specs=(P(("dom", "fsdp"), None), P("fsdp", None), P("fsdp")),
        check_vma=False,
    )
```

```python
import functools

import jax
import jax.numpy as jnp
import numpy as np
from jax import lax
from jax.experimental import pallas as pl
from jax.experimental.pallas import tpu as pltpu
from jax.sharding import PartitionSpec as P

HD = 128
HALF = HD // 2
BLOCK = 128
LANES = 128
MESH = pl.DeviceIdType.MESH
F32 = jnp.float32
BF16 = jnp.bfloat16


def to_column(row, size):
    eye = lax.broadcasted_iota(jnp.int32, (size, size), 0) == lax.broadcasted_iota(
        jnp.int32, (size, size), 1
    )
    return jnp.sum(jnp.where(eye, row, jnp.float32(0.0)), axis=1, keepdims=True)


def to_row(column, size):
    eye = lax.broadcasted_iota(jnp.int32, (size, size), 0) == lax.broadcasted_iota(
        jnp.int32, (size, size), 1
    )
    return jnp.sum(jnp.where(eye, column, jnp.float32(0.0)), axis=0, keepdims=True)


def kernel(
    ny,
    nz,
    counts_hbm,
    ratios_hbm,
    gain_hbm,
    weight_hbm,
    positions_hbm,
    freq_hbm,
    tokens_hbm,
    cot_hbm,
    kv_ref,
    wg_ref,
    gg_ref,
    counts_ref,
    ratios_ref,
    gain_ref,
    weight_ref,
    positions_ref,
    freq_ref,
    tokens_ref,
    cot_ref,
    own_gw,
    land_g1,
    piece_g,
    full_gw,
    part_m,
    land_r0,
    sum_r0,
    land_r1,
    sum_r1,
    land_r2,
    sum_r2,
    land_r3,
    upstream,
    sem_in,
    sem_g1s,
    sem_g1r,
    sem_gxs,
    sem_gxr,
    sem_g2s,
    sem_g2r,
    sem_g3s,
    sem_g3r,
    sem_r0s,
    sem_r0r,
    sem_r1s,
    sem_r1r,
    sem_r2s,
    sem_r2r,
    sem_r3s,
    sem_r3r,
    sem_in_ring,
    sem_in_far,
):
    dom = lax.axis_index("dom")
    fsdp = lax.axis_index("fsdp")
    core = lax.rem(dom, 2)
    y = lax.rem(lax.div(dom, 2), ny)
    x_hi = lax.div(dom, 2 * ny)
    z = lax.div(fsdp, 2)
    x_lo = lax.rem(fsdp, 2)
    x = x_hi * 2 + x_lo
    q = x_hi * 2 + core
    jn = nz // 8
    plane = 4 * ny
    steps = 2 * jn
    rows, width = tokens_ref.shape
    shard, cols = weight_ref.shape
    slab = 2 * shard
    key_width = cols // 2
    heads = key_width // HD
    group = 8 * slab
    lo_own = lax.rem(z + core, 2)
    lo_sib = 1 - lo_own

    def dev(xx, yy, cc, zz):
        return (lax.div(xx, 2) * (2 * ny) + yy * 2 + cc, zz * 2 + lax.rem(xx, 2))

    def remote(src, dst, send, recv, device):
        return pltpu.make_async_remote_copy(
            src_ref=src,
            dst_ref=dst,
            send_sem=send,
            recv_sem=recv,
            device_id=device,
            device_id_type=MESH,
        )

    def lane_tile(i):
        return pl.ds(pl.multiple_of(i * LANES, LANES), LANES)

    def wrap_z(value):
        return lax.rem(value + 2 * nz, nz)

    loads = [
        pltpu.make_async_copy(src, dst, sem_in.at[i])
        for i, (src, dst) in enumerate(
            (
                (tokens_hbm, tokens_ref),
                (cot_hbm, cot_ref),
                (positions_hbm, positions_ref),
                (freq_hbm, freq_ref),
                (weight_hbm, weight_ref),
                (gain_hbm, gain_ref),
                (counts_hbm, counts_ref),
                (ratios_hbm, ratios_ref),
            )
        )
    ]
    for load in loads:
        load.start()

    own_class = q + 4 * x_lo
    own_shift = q - 4 * x_lo
    residue = lax.rem(z - own_class + 2 * nz, 8)
    hi_own = lax.div(residue, 2)
    home = lax.div(wrap_z(z - own_shift), 8)

    barrier = pltpu.get_barrier_semaphore()

    def greet(device):
        pl.semaphore_signal(barrier, inc=1, device_id=device, device_id_type=MESH)

    xs = [lax.rem(x + i, 4) for i in range(4)]
    ys = [lax.rem(y + i, ny) for i in range(ny)]

    def class_of(xx, cc):
        return lax.div(xx, 2) * 2 + cc + 4 * lax.rem(xx, 2)

    def hi_of(xx, cc):
        return lax.div(lax.rem(z - class_of(xx, cc) + 2 * nz, 8), 2)

    his = [hi_of(xx, core) for xx in xs]
    at_plane = [[dev(xx, yy, core, z) for yy in ys] for xx in xs]
    at_other = [[(a + 1 - 2 * core, b) for a, b in line] for line in at_plane]
    sibling = at_other[0][0]
    peers = [(i, j) for i in range(4) for j in range(ny)][1:]
    peers.sort(key=lambda p: (min(p[0], 4 - p[0]) + min(p[1], ny - p[1]), sum(p)))

    greet(sibling)
    for i, j in peers:
        greet(at_plane[i][j])
        if i % 2 == 0:
            greet(at_other[i][j])
    near_self = (own_class == 0).astype(jnp.int32)
    for half in range(2):
        owner = dev(x_hi * 2 + half, y, core, wrap_z(z - own_shift))
        if half == 0:

            @pl.when(own_class != 0)
            def _(owner=owner):
                greet(owner)

        else:
            greet(owner)
    for t in range(2):
        near = dev(x_hi * 2 + t, y, core, wrap_z(z + q - 4 * t))
        if t == 0:

            @pl.when(own_class != 0)
            def _(near=near):
                greet(near)

        else:
            greet(near)
    ring = min(jn - 1, 2)
    ahead = dev(x, y, core, wrap_z(z + 8))
    behind = dev(x, y, core, wrap_z(z - 8))
    if jn > 1:
        greet(ahead)
    if jn > 2:
        greet(behind)

    loads[4].wait()
    loads[5].wait()
    gain_col = to_column(gain_ref[...].astype(F32), shard)
    weight = weight_ref[...].astype(F32)
    own_gw[...] = (weight * gain_col).astype(BF16)

    loads[2].wait()
    loads[3].wait()
    pos = positions_ref[...].astype(F32)
    pos_col = jnp.concatenate(
        [to_column(pos[i : i + 1, :], LANES) for i in range(rows // LANES)], axis=0
    )
    angles = pos_col * freq_ref[...]
    cosines = jnp.cos(angles)
    lane_ids = lax.broadcasted_iota(jnp.int32, (rows, HD), 1)
    sines = jnp.where(lane_ids < HALF, -1.0, 1.0) * jnp.sin(angles)

    loads[6].wait()
    loads[7].wait()
    counts = counts_ref[...].astype(F32)
    n_dom, n_mem = counts.shape
    domain_rows = BLOCK * jnp.sum(counts, axis=1, keepdims=True)
    live_total = jnp.sum(domain_rows, axis=0, keepdims=True)
    ratio = to_column(ratios_ref[...].astype(F32), n_dom)
    factor = ratio / jnp.sum(ratio, axis=0, keepdims=True) * live_total / domain_rows
    dom_ids = lax.broadcasted_iota(jnp.int32, (n_dom, 1), 0)
    own_factor = jnp.sum(jnp.where(dom_ids == dom, factor, 0.0), axis=0, keepdims=True)
    at_dom = lax.broadcasted_iota(jnp.int32, (n_dom, n_mem), 0) == dom
    at_mem = lax.broadcasted_iota(jnp.int32, (n_dom, n_mem), 1) == fsdp
    own_count = jnp.sum(
        jnp.sum(jnp.where(at_dom & at_mem, counts, 0.0), axis=1, keepdims=True),
        axis=0,
        keepdims=True,
    )
    row_ids = lax.broadcasted_iota(jnp.int32, (rows, 1), 0).astype(F32)
    row_factor = jnp.where(row_ids < BLOCK * own_count, own_factor, 0.0)

    loads[0].wait()
    token = tokens_ref[...].astype(F32)
    mean_square = jnp.sum(token * token, axis=1, keepdims=True) * (1.0 / width)
    inv_norm = lax.rsqrt(mean_square + 1e-06)

    loads[1].wait()
    scale = row_factor * inv_norm
    for h in range(2 * heads):
        part = cot_ref[:, h * HD : (h + 1) * HD].astype(F32) * scale
        if h < heads:
            part = part * cosines - pltpu.roll(part, HALF, 1) * sines
        upstream[:, h * HD : (h + 1) * HD] = part.astype(BF16)

    pl.semaphore_wait(barrier, plane + plane // 2 - 1 + 4 + ring - 2 * near_self)

    def tell(sem, device):
        pl.semaphore_signal(sem, inc=1, device_id=device, device_id_type=MESH)

    if jn > 1:
        tell(sem_in_ring, ahead)
    if jn > 2:
        tell(sem_in_ring, behind)

    def g1_copy(t):
        return remote(
            own_gw.at[:, lane_tile(y)],
            land_g1.at[x_lo],
            sem_g1s.at[t],
            sem_g1r.at[x_lo],
            dev(x_hi * 2 + t, y, core, wrap_z(z + q - 4 * t)),
        )

    g1_local = pltpu.make_async_copy(
        own_gw.at[:, lane_tile(y)], land_g1.at[0], sem_g1r.at[0]
    )

    @pl.when(own_class != 0)
    def _():
        g1_copy(0).start()

    @pl.when(own_class == 0)
    def _():
        g1_local.start()

    g1_copy(1).start()

    def r0_copy(j):
        return remote(
            part_m.at[j, :, lo_sib], land_r0.at[j], sem_r0s, sem_r0r.at[j], sibling
        )

    def m_step(j, carry):
        lhs = tokens_ref[:, pl.ds(pl.multiple_of(j * group, group), group)]
        prod = lax.dot_general(
            lhs, upstream[...], (((0,), (0,)), ((), ())), preferred_element_type=F32
        )
        part_m[j] = prod.reshape(4, 2, slab, cols).astype(BF16)
        r0_copy(j).start()
        return carry

    def r1_send(j, carry):
        r0_copy(j).wait_recv()
        total = part_m[j, :, lo_own].astype(F32) + land_r0[j].astype(F32)
        sum_r0[j] = total.astype(BF16)
        for k, (dx, dy) in enumerate(peers):
            remote(
                sum_r0.at[j, his[dx], :, lane_tile(ys[dy])],
                land_r1.at[j, k],
                sem_r1s,
                sem_r1r.at[j],
                at_plane[dx][dy],
            ).start()
        return carry

    m_step(0, 0)

    def m_and_r1(j, carry):
        m_step(j, carry)
        return r1_send(j - 1, carry)

    lax.fori_loop(1, jn, m_and_r1, 0)

    for half in range(2):
        pltpu.make_async_copy(
            land_g1.at[half], land_g1.at[half], sem_g1r.at[half]
        ).wait()
    piece_g[home] = jnp.concatenate(
        [land_g1[0].astype(F32), land_g1[1].astype(F32)], axis=0
    ).astype(BF16)

    def ring_copy(i, at, device):
        return remote(
            piece_g.at[at], piece_g.at[at], sem_gxs.at[i], sem_gxr.at[i], device
        )

    def nth(i):
        return lax.rem(home + i + 2 * jn, jn)

    if jn > 1:
        ring_copy(0, home, ahead).start()
    if jn > 2:
        ring_copy(1, home, behind).start()

    r1_send(jn - 1, 0)
    if jn > 1:
        pl.semaphore_wait(sem_in_ring, ring)
    if jn > 3:
        tell(sem_in_far, ahead)

    def arrived(buffer, sem):
        pltpu.make_async_copy(buffer, buffer, sem).wait()

    def r1_arrive(j, carry):
        arrived(land_r1.at[j], sem_r1r.at[j])
        total = sum_r0[j, hi_own, :, lane_tile(y)].astype(F32)
        for k in range(plane - 1):
            total = total + land_r1[j, k].astype(F32)
        for half in range(2):
            sum_r1[j, half] = total[half * shard : (half + 1) * shard, :].astype(BF16)
        return carry

    def r2_copy(j, half):
        far = 8 * j + residue
        slot = 2 * lax.div(wrap_z(z - own_class - far), 8) + x_lo
        return remote(
            sum_r1.at[j, half],
            land_r2.at[slot],
            sem_r2s,
            sem_r2r,
            dev(x_hi * 2 + half, y, core, far),
        )

    def r2_send(j, carry):
        stays = (own_class == 0) & (j == home)

        @pl.when(jnp.logical_not(stays))
        def _():
            r2_copy(j, 0).start()

        @pl.when(stays)
        def _():
            pltpu.make_async_copy(sum_r1.at[j, 0], land_r2.at[0], sem_r2r).start()

        r2_copy(j, 1).start()
        return carry

    def r1_and_r2(j, carry):
        r1_arrive(j, carry)
        return r2_send(j, carry)

    early = min(2, jn)
    lax.fori_loop(0, early, r1_arrive, 0)
    if jn > 1:
        ring_copy(0, nth(-1), behind).wait_recv()
    if jn > 3:
        ring_copy(2, nth(-1), ahead).start()
        pl.semaphore_wait(sem_in_far, 1)
    lax.fori_loop(0, early, r2_send, 0)
    lax.fori_loop(early, jn, r1_and_r2, 0)
    if jn > 2:
        ring_copy(1, nth(1), ahead).wait_recv()
    if jn > 3:
        ring_copy(2, nth(2), behind).wait_recv()

    g2_view = full_gw.at[:, hi_own, lo_own, :, lane_tile(y)]
    pltpu.make_async_copy(piece_g, g2_view, sem_g2r.at[0]).start()
    for dx, dy in peers:
        remote(piece_g, g2_view, sem_g2s, sem_g2r.at[dx], at_plane[dx][dy]).start()

    arrived(land_r0, sem_r0s)
    arrived(land_r1, sem_r1s)

    @pl.when(own_class != 0)
    def _():
        g1_copy(0).wait_send()

    g1_copy(1).wait_send()
    for i in range(min(jn - 1, 3)):
        ring_copy(i, home, ahead).wait_send()

    arrived(land_r2, sem_r2r)
    total2 = land_r2[0].astype(F32)
    for s in range(1, steps):
        total2 = total2 + land_r2[s].astype(F32)
    sum_r2[...] = total2

    slot3 = 4 * y + q
    pltpu.make_async_copy(sum_r2, land_r3.at[slot3], sem_r3r).start()

    def r3_send(device):
        remote(sum_r2, land_r3.at[slot3], sem_r3s, sem_r3r, device).start()

    r3_send(sibling)
    for dx in (0, 2):
        for dy in range(ny):
            if dx or dy:
                r3_send(at_plane[dx][dy])
                r3_send(at_other[dx][dy])

    def g3_copy(hi, lo, i):
        view = full_gw.at[:, hi, lo]
        return remote(view, view, sem_g3s, sem_g3r.at[i], sibling)

    for dx in range(4):
        back = (4 - dx) % 4
        arrived(full_gw.at[:, his[back], lo_own], sem_g2r.at[dx])
        g3_copy(his[back], lo_own, dx).start()

    for dx in range(4):
        back = (4 - dx) % 4
        arrived(full_gw.at[:, hi_of(xs[back], 1 - core), lo_sib], sem_g3r.at[dx])

    def p_step(j, total):
        lhs = tokens_ref[:, pl.ds(pl.multiple_of(j * group, group), group)]
        rhs = full_gw[j].reshape(group, cols)
        return total + jnp.dot(lhs, rhs, preferred_element_type=F32)

    projected = lax.fori_loop(0, jn, p_step, jnp.zeros((rows, cols), F32))
    projected = projected * inv_norm
    for h in range(2 * heads):
        part = projected[:, h * HD : (h + 1) * HD]
        if h < heads:
            part = part * cosines + pltpu.roll(part, HALF, 1) * sines
        kv_ref[:, h * HD : (h + 1) * HD] = part.astype(BF16)

    arrived(land_r3, sem_r3r)
    root = jnp.sqrt(live_total)
    gain_sum = jnp.zeros((shard, 1), F32)
    for i in range(ny):
        tile = slice(i * LANES, (i + 1) * LANES)
        total3 = land_r3[4 * i] + land_r3[4 * i + 1] + land_r3[4 * i + 2] + land_r3[4 * i + 3]
        wg_ref[:, tile] = total3 * gain_col / root
        gain_sum = gain_sum + jnp.sum(total3 * weight[:, tile], axis=1, keepdims=True)
    gg_ref[...] = to_row(gain_sum / root, shard)

    arrived(land_r1, sem_g2s)
    arrived(full_gw.at[:, :, lo_own], sem_g3s)

    @pl.when(own_class != 0)
    def _():
        arrived(land_r2, sem_r2s)

    @pl.when(own_class == 0)
    def _():
        arrived(land_r2.at[pl.ds(0, steps - 1)], sem_r2s)

    arrived(land_r3.at[pl.ds(0, plane - 1)], sem_r3s)


def copy_kernel(count, *refs):
    sems = refs[-1]
    copies = [
        pltpu.make_async_copy(refs[i], refs[count + i], sems.at[i])
        for i in range(count)
    ]
    for copy in copies:
        copy.start()
    for copy in copies:
        copy.wait()


def body(ny, nz, tokens, gain, kv_weight, positions, cotangent, counts, ratios):
    rows, width = tokens.shape
    shard, cols = kv_weight.shape
    jn, plane = nz // 8, 4 * ny
    steps = 2 * jn
    slab = 2 * shard
    exponents = np.arange(HALF) * (2.0 / HD)
    freq = np.power(1000000.0, -exponents).astype(np.float32)
    freq = jnp.asarray(np.concatenate([freq, freq])[None, :])
    operands = (
        counts,
        ratios.reshape(1, -1),
        gain.reshape(1, -1),
        kv_weight,
        positions.reshape(-1, LANES),
        freq,
        tokens,
        cotangent,
    )
    hbm = pl.BlockSpec(memory_space=pltpu.HBM)
    vmem = pl.BlockSpec(memory_space=pltpu.VMEM)
    dma = pltpu.SemaphoreType.DMA
    shapes = (
        jax.ShapeDtypeStruct((rows, cols), BF16),
        jax.ShapeDtypeStruct((shard, cols), F32),
        jax.ShapeDtypeStruct((1, shard), F32),
    )
    outs = pl.pallas_call(
        functools.partial(kernel, ny, nz),
        out_shape=shapes,
        in_specs=[hbm] * len(operands),
        out_specs=(vmem, vmem, vmem),
        scratch_shapes=[pltpu.VMEM(v.shape, v.dtype) for v in operands]
        + [
            pltpu.VMEM((shard, cols), BF16),
            pltpu.VMEM((2, shard, LANES), BF16),
            pltpu.VMEM((jn, slab, LANES), BF16),
            pltpu.VMEM((jn, 4, 2, slab, cols), BF16),
            pltpu.VMEM((jn, 4, 2, slab, cols), BF16),
            pltpu.VMEM((jn, 4, slab, cols), BF16),
            pltpu.VMEM((jn, 4, slab, cols), BF16),
            pltpu.VMEM((jn, plane - 1, slab, LANES), BF16),
            pltpu.VMEM((jn, 2, shard, LANES), BF16),
            pltpu.VMEM((steps, shard, LANES), BF16),
            pltpu.VMEM((shard, LANES), F32),
            pltpu.VMEM((plane, shard, LANES), F32),
            pltpu.VMEM((rows, cols), BF16),
            dma((len(operands),)),
            dma((2,)),
            dma((2,)),
            dma((3,)),
            dma((3,)),
            dma,
            dma((4,)),
            dma,
            dma((4,)),
            dma,
            dma((jn,)),
            dma,
            dma((jn,)),
            dma,
            dma,
            dma,
            dma,
            pltpu.SemaphoreType.REGULAR,
            pltpu.SemaphoreType.REGULAR,
        ],
        compiler_params=pltpu.CompilerParams(
            collective_id=0, has_side_effects=True, vmem_limit_bytes=40 * 2**20
        ),
        name="kv_exchange",
    )(*[pltpu.with_memory_space_constraint(v, pltpu.HBM) for v in operands])
    kv, wg, gg = pl.pallas_call(
        functools.partial(copy_kernel, len(outs)),
        out_shape=shapes,
        in_specs=[vmem] * len(outs),
        out_specs=(hbm, hbm, hbm),
        scratch_shapes=[dma((len(outs),))],
        name="kv_outputs",
    )(*[pltpu.with_memory_space_constraint(v, pltpu.VMEM) for v in outs])
    return (kv, wg, gg.reshape(-1))


def solution(mesh):
    ny = mesh.shape["dom"] // 4
    nz = mesh.shape["fsdp"] // 2
    return jax.shard_map(
        functools.partial(body, ny, nz),
        mesh=mesh,
        in_specs=(
            P(("dom", "fsdp"), None),
            P("fsdp"),
            P("fsdp", None),
            P(("dom", "fsdp")),
            P(("dom", "fsdp"), None),
            P(),
            P(),
        ),
        out_specs=(P(("dom", "fsdp"), None), P("fsdp", None), P("fsdp")),
        check_vma=False,
    )
```

```python
import functools

import jax
import jax.numpy as jnp
import numpy as np
from jax import lax
from jax.experimental import pallas as pl
from jax.experimental.pallas import tpu as pltpu
from jax.sharding import PartitionSpec as P

HD = 128
HALF = HD // 2
BLOCK = 128
LANES = 128
MESH = pl.DeviceIdType.MESH
F32 = jnp.float32
BF16 = jnp.bfloat16


def to_column(row, size):
    eye = lax.broadcasted_iota(jnp.int32, (size, size), 0) == lax.broadcasted_iota(
        jnp.int32, (size, size), 1
    )
    return jnp.sum(jnp.where(eye, row, jnp.float32(0.0)), axis=1, keepdims=True)


def to_row(column, size):
    eye = lax.broadcasted_iota(jnp.int32, (size, size), 0) == lax.broadcasted_iota(
        jnp.int32, (size, size), 1
    )
    return jnp.sum(jnp.where(eye, column, jnp.float32(0.0)), axis=0, keepdims=True)


def kernel(
    ny,
    nz,
    counts_hbm,
    ratios_hbm,
    gain_hbm,
    weight_hbm,
    positions_hbm,
    freq_hbm,
    tokens_hbm,
    cot_hbm,
    kv_ref,
    wg_ref,
    gg_ref,
    counts_ref,
    ratios_ref,
    gain_ref,
    weight_ref,
    positions_ref,
    freq_ref,
    tokens_ref,
    cot_ref,
    own_gw,
    land_g1,
    piece_g,
    full_gw,
    part_m,
    land_r0,
    sum_r0,
    land_r1,
    sum_r1,
    land_r2,
    sum_r2,
    land_r3,
    upstream,
    sem_in,
    sem_g1s,
    sem_g1r,
    sem_gxs,
    sem_gxr,
    sem_g2s,
    sem_g2r,
    sem_g3s,
    sem_g3r,
    sem_r0s,
    sem_r0r,
    sem_r1s,
    sem_r1r,
    sem_r2s,
    sem_r2r,
    sem_r3s,
    sem_r3r,
    sem_in_ring,
    sem_in_far,
):
    dom = lax.axis_index("dom")
    fsdp = lax.axis_index("fsdp")
    core = lax.rem(dom, 2)
    y = lax.rem(lax.div(dom, 2), ny)
    x_hi = lax.div(dom, 2 * ny)
    z = lax.div(fsdp, 2)
    x_lo = lax.rem(fsdp, 2)
    x = x_hi * 2 + x_lo
    q = x_hi * 2 + core
    jn = nz // 8
    plane = 4 * ny
    steps = 2 * jn
    rows, width = tokens_ref.shape
    shard, cols = weight_ref.shape
    slab = 2 * shard
    key_width = cols // 2
    heads = key_width // HD
    group = 8 * slab
    lo_own = lax.rem(z + core, 2)
    lo_sib = 1 - lo_own

    def dev(xx, yy, cc, zz):
        return (lax.div(xx, 2) * (2 * ny) + yy * 2 + cc, zz * 2 + lax.rem(xx, 2))

    def remote(src, dst, send, recv, device):
        return pltpu.make_async_remote_copy(
            src_ref=src,
            dst_ref=dst,
            send_sem=send,
            recv_sem=recv,
            device_id=device,
            device_id_type=MESH,
        )

    def lane_tile(i):
        return pl.ds(pl.multiple_of(i * LANES, LANES), LANES)

    def wrap_z(value):
        return lax.rem(value + 2 * nz, nz)

    loads = [
        pltpu.make_async_copy(src, dst, sem_in.at[i])
        for i, (src, dst) in enumerate(
            (
                (tokens_hbm, tokens_ref),
                (cot_hbm, cot_ref),
                (positions_hbm, positions_ref),
                (freq_hbm, freq_ref),
                (weight_hbm, weight_ref),
                (gain_hbm, gain_ref),
                (counts_hbm, counts_ref),
                (ratios_hbm, ratios_ref),
            )
        )
    ]
    for load in loads:
        load.start()

    own_class = q + 4 * x_lo
    own_shift = q - 4 * x_lo
    residue = lax.rem(z - own_class + 2 * nz, 8)
    hi_own = lax.div(residue, 2)
    home = lax.div(wrap_z(z - own_shift), 8)

    barrier = pltpu.get_barrier_semaphore()

    def greet(device):
        pl.semaphore_signal(barrier, inc=1, device_id=device, device_id_type=MESH)

    xs = [lax.rem(x + i, 4) for i in range(4)]
    ys = [lax.rem(y + i, ny) for i in range(ny)]

    def class_of(xx, cc):
        return lax.div(xx, 2) * 2 + cc + 4 * lax.rem(xx, 2)

    def hi_of(xx, cc):
        return lax.div(lax.rem(z - class_of(xx, cc) + 2 * nz, 8), 2)

    his = [hi_of(xx, core) for xx in xs]
    at_plane = [[dev(xx, yy, core, z) for yy in ys] for xx in xs]
    at_other = [[(a + 1 - 2 * core, b) for a, b in line] for line in at_plane]
    sibling = at_other[0][0]
    peers = [(i, j) for i in range(4) for j in range(ny)][1:]
    peers.sort(key=lambda p: (min(p[0], 4 - p[0]) + min(p[1], ny - p[1]), sum(p)))

    greet(sibling)
    for i, j in peers:
        greet(at_plane[i][j])
        if i % 2 == 0:
            greet(at_other[i][j])
    near_self = (own_class == 0).astype(jnp.int32)
    for half in range(2):
        owner = dev(x_hi * 2 + half, y, core, wrap_z(z - own_shift))
        if half == 0:

            @pl.when(own_class != 0)
            def _(owner=owner):
                greet(owner)

        else:
            greet(owner)
    for t in range(2):
        near = dev(x_hi * 2 + t, y, core, wrap_z(z + q - 4 * t))
        if t == 0:

            @pl.when(own_class != 0)
            def _(near=near):
                greet(near)

        else:
            greet(near)
    ring = min(jn - 1, 2)
    ahead = dev(x, y, core, wrap_z(z + 8))
    behind = dev(x, y, core, wrap_z(z - 8))
    if jn > 1:
        greet(ahead)
    if jn > 2:
        greet(behind)

    loads[4].wait()
    loads[5].wait()
    gain_col = to_column(gain_ref[...].astype(F32), shard)
    weight = weight_ref[...].astype(F32)
    own_gw[...] = (weight * gain_col).astype(BF16)

    loads[2].wait()
    loads[3].wait()
    pos = positions_ref[...].astype(F32)
    pos_col = jnp.concatenate(
        [to_column(pos[i : i + 1, :], LANES) for i in range(rows // LANES)], axis=0
    )
    angles = pos_col * freq_ref[...]
    cosines = jnp.cos(angles)
    lane_ids = lax.broadcasted_iota(jnp.int32, (rows, HD), 1)
    sines = jnp.where(lane_ids < HALF, -1.0, 1.0) * jnp.sin(angles)

    loads[6].wait()
    loads[7].wait()
    counts = counts_ref[...].astype(F32)
    n_dom, n_mem = counts.shape
    domain_rows = BLOCK * jnp.sum(counts, axis=1, keepdims=True)
    live_total = jnp.sum(domain_rows, axis=0, keepdims=True)
    ratio = to_column(ratios_ref[...].astype(F32), n_dom)
    factor = ratio / jnp.sum(ratio, axis=0, keepdims=True) * live_total / domain_rows
    dom_ids = lax.broadcasted_iota(jnp.int32, (n_dom, 1), 0)
    own_factor = jnp.sum(jnp.where(dom_ids == dom, factor, 0.0), axis=0, keepdims=True)
    at_dom = lax.broadcasted_iota(jnp.int32, (n_dom, n_mem), 0) == dom
    at_mem = lax.broadcasted_iota(jnp.int32, (n_dom, n_mem), 1) == fsdp
    own_count = jnp.sum(
        jnp.sum(jnp.where(at_dom & at_mem, counts, 0.0), axis=1, keepdims=True),
        axis=0,
        keepdims=True,
    )
    row_ids = lax.broadcasted_iota(jnp.int32, (rows, 1), 0).astype(F32)
    row_factor = jnp.where(row_ids < BLOCK * own_count, own_factor, 0.0)

    loads[0].wait()
    token = tokens_ref[...].astype(F32)
    mean_square = jnp.sum(token * token, axis=1, keepdims=True) * (1.0 / width)
    inv_norm = lax.rsqrt(mean_square + 1e-06)

    loads[1].wait()
    scale = row_factor * inv_norm
    for h in range(2 * heads):
        part = cot_ref[:, h * HD : (h + 1) * HD].astype(F32) * scale
        if h < heads:
            part = part * cosines - pltpu.roll(part, HALF, 1) * sines
        upstream[:, h * HD : (h + 1) * HD] = part.astype(BF16)

    pl.semaphore_wait(barrier, plane + plane // 2 - 1 + 4 + ring - 2 * near_self)

    def tell(sem, device):
        pl.semaphore_signal(sem, inc=1, device_id=device, device_id_type=MESH)

    if jn > 1:
        tell(sem_in_ring, ahead)
    if jn > 2:
        tell(sem_in_ring, behind)

    def g1_copy(t):
        return remote(
            own_gw.at[:, lane_tile(y)],
            land_g1.at[x_lo],
            sem_g1s.at[t],
            sem_g1r.at[x_lo],
            dev(x_hi * 2 + t, y, core, wrap_z(z + q - 4 * t)),
        )

    g1_local = pltpu.make_async_copy(
        own_gw.at[:, lane_tile(y)], land_g1.at[0], sem_g1r.at[0]
    )

    @pl.when(own_class != 0)
    def _():
        g1_copy(0).start()

    @pl.when(own_class == 0)
    def _():
        g1_local.start()

    g1_copy(1).start()

    def r0_copy(j):
        return remote(
            part_m.at[j, :, lo_sib], land_r0.at[j], sem_r0s, sem_r0r.at[j], sibling
        )

    def m_step(j, carry):
        lhs = tokens_ref[:, pl.ds(pl.multiple_of(j * group, group), group)]
        prod = lax.dot_general(
            lhs, upstream[...], (((0,), (0,)), ((), ())), preferred_element_type=F32
        )
        part_m[j] = prod.reshape(4, 2, slab, cols).astype(BF16)
        r0_copy(j).start()
        return carry

    def r1_send(j, carry):
        r0_copy(j).wait_recv()
        total = part_m[j, :, lo_own].astype(F32) + land_r0[j].astype(F32)
        sum_r0[j] = total.astype(BF16)
        for k, (dx, dy) in enumerate(peers):
            remote(
                sum_r0.at[j, his[dx], :, lane_tile(ys[dy])],
                land_r1.at[j, k],
                sem_r1s,
                sem_r1r.at[j],
                at_plane[dx][dy],
            ).start()
        return carry

    m_step(0, 0)

    def m_and_r1(j, carry):
        m_step(j, carry)
        return r1_send(j - 1, carry)

    lax.fori_loop(1, jn, m_and_r1, 0)

    for half in range(2):
        pltpu.make_async_copy(
            land_g1.at[half], land_g1.at[half], sem_g1r.at[half]
        ).wait()
    piece_g[home] = jnp.concatenate(
        [land_g1[0].astype(F32), land_g1[1].astype(F32)], axis=0
    ).astype(BF16)

    def ring_copy(i, at, device):
        return remote(
            piece_g.at[at], piece_g.at[at], sem_gxs.at[i], sem_gxr.at[i], device
        )

    def nth(i):
        return lax.rem(home + i + 2 * jn, jn)

    if jn > 1:
        ring_copy(0, home, ahead).start()
    if jn > 2:
        ring_copy(1, home, behind).start()

    r1_send(jn - 1, 0)
    if jn > 1:
        pl.semaphore_wait(sem_in_ring, ring)
    if jn > 3:
        tell(sem_in_far, ahead)

    def arrived(buffer, sem):
        pltpu.make_async_copy(buffer, buffer, sem).wait()

    def r1_arrive(j, carry):
        arrived(land_r1.at[j], sem_r1r.at[j])
        total = sum_r0[j, hi_own, :, lane_tile(y)].astype(F32)
        for k in range(plane - 1):
            total = total + land_r1[j, k].astype(F32)
        for half in range(2):
            sum_r1[j, half] = total[half * shard : (half + 1) * shard, :].astype(BF16)
        return carry

    def r2_copy(j, half):
        far = 8 * j + residue
        slot = 2 * lax.div(wrap_z(z - own_class - far), 8) + x_lo
        return remote(
            sum_r1.at[j, half],
            land_r2.at[slot],
            sem_r2s,
            sem_r2r,
            dev(x_hi * 2 + half, y, core, far),
        )

    def r2_send(j, carry):
        stays = (own_class == 0) & (j == home)

        @pl.when(jnp.logical_not(stays))
        def _():
            r2_copy(j, 0).start()

        @pl.when(stays)
        def _():
            pltpu.make_async_copy(sum_r1.at[j, 0], land_r2.at[0], sem_r2r).start()

        r2_copy(j, 1).start()
        return carry

    def r1_and_r2(j, carry):
        r1_arrive(j, carry)
        return r2_send(j, carry)

    early = min(2, jn)
    lax.fori_loop(0, early, r1_arrive, 0)
    if jn > 1:
        ring_copy(0, nth(-1), behind).wait_recv()
    if jn > 3:
        ring_copy(2, nth(-1), ahead).start()
        pl.semaphore_wait(sem_in_far, 1)
    lax.fori_loop(0, early, r2_send, 0)
    lax.fori_loop(early, jn, r1_and_r2, 0)
    def g2_send(i):
        at = nth(i)
        view = full_gw.at[at, hi_own, lo_own, :, lane_tile(y)]
        for dx, dy in peers:
            remote(
                piece_g.at[at], view, sem_g2s, sem_g2r.at[dx], at_plane[dx][dy]
            ).start()
        pltpu.make_async_copy(piece_g.at[at], view, sem_g2r.at[0]).start()

    g2_send(0)
    if jn > 1:
        g2_send(-1)
    if jn > 2:
        ring_copy(1, nth(1), ahead).wait_recv()
        g2_send(1)
    if jn > 3:
        ring_copy(2, nth(2), behind).wait_recv()
        g2_send(2)

    arrived(land_r0, sem_r0s)
    arrived(land_r1, sem_r1s)

    @pl.when(own_class != 0)
    def _():
        g1_copy(0).wait_send()

    g1_copy(1).wait_send()
    for i in range(min(jn - 1, 3)):
        ring_copy(i, home, ahead).wait_send()

    arrived(land_r2, sem_r2r)
    total2 = land_r2[0].astype(F32)
    for s in range(1, steps):
        total2 = total2 + land_r2[s].astype(F32)
    sum_r2[...] = total2

    slot3 = 4 * y + q
    pltpu.make_async_copy(sum_r2, land_r3.at[slot3], sem_r3r).start()

    def r3_send(device):
        remote(sum_r2, land_r3.at[slot3], sem_r3s, sem_r3r, device).start()

    r3_send(sibling)
    for dx in (0, 2):
        for dy in range(ny):
            if dx or dy:
                r3_send(at_plane[dx][dy])
                r3_send(at_other[dx][dy])

    def g3_copy(hi, lo, i):
        view = full_gw.at[:, hi, lo]
        return remote(view, view, sem_g3s, sem_g3r.at[i], sibling)

    for dx in range(4):
        back = (4 - dx) % 4
        arrived(full_gw.at[:, his[back], lo_own], sem_g2r.at[dx])
        g3_copy(his[back], lo_own, dx).start()

    for dx in range(4):
        back = (4 - dx) % 4
        arrived(full_gw.at[:, hi_of(xs[back], 1 - core), lo_sib], sem_g3r.at[dx])

    def p_step(j, total):
        lhs = tokens_ref[:, pl.ds(pl.multiple_of(j * group, group), group)]
        rhs = full_gw[j].reshape(group, cols)
        return total + jnp.dot(lhs, rhs, preferred_element_type=F32)

    projected = lax.fori_loop(0, jn, p_step, jnp.zeros((rows, cols), F32))
    projected = projected * inv_norm
    for h in range(2 * heads):
        part = projected[:, h * HD : (h + 1) * HD]
        if h < heads:
            part = part * cosines + pltpu.roll(part, HALF, 1) * sines
        kv_ref[:, h * HD : (h + 1) * HD] = part.astype(BF16)

    arrived(land_r3, sem_r3r)
    root = jnp.sqrt(live_total)
    gain_sum = jnp.zeros((shard, 1), F32)
    for i in range(ny):
        tile = slice(i * LANES, (i + 1) * LANES)
        total3 = land_r3[4 * i] + land_r3[4 * i + 1] + land_r3[4 * i + 2] + land_r3[4 * i + 3]
        wg_ref[:, tile] = total3 * gain_col / root
        gain_sum = gain_sum + jnp.sum(total3 * weight[:, tile], axis=1, keepdims=True)
    gg_ref[...] = to_row(gain_sum / root, shard)

    arrived(land_r1, sem_g2s)
    arrived(full_gw.at[:, :, lo_own], sem_g3s)

    @pl.when(own_class != 0)
    def _():
        arrived(land_r2, sem_r2s)

    @pl.when(own_class == 0)
    def _():
        arrived(land_r2.at[pl.ds(0, steps - 1)], sem_r2s)

    arrived(land_r3.at[pl.ds(0, plane - 1)], sem_r3s)


def copy_kernel(count, *refs):
    sems = refs[-1]
    copies = [
        pltpu.make_async_copy(refs[i], refs[count + i], sems.at[i])
        for i in range(count)
    ]
    for copy in copies:
        copy.start()
    for copy in copies:
        copy.wait()


def body(ny, nz, tokens, gain, kv_weight, positions, cotangent, counts, ratios):
    rows, width = tokens.shape
    shard, cols = kv_weight.shape
    jn, plane = nz // 8, 4 * ny
    steps = 2 * jn
    slab = 2 * shard
    exponents = np.arange(HALF) * (2.0 / HD)
    freq = np.power(1000000.0, -exponents).astype(np.float32)
    freq = jnp.asarray(np.concatenate([freq, freq])[None, :])
    operands = (
        counts,
        ratios.reshape(1, -1),
        gain.reshape(1, -1),
        kv_weight,
        positions.reshape(-1, LANES),
        freq,
        tokens,
        cotangent,
    )
    hbm = pl.BlockSpec(memory_space=pltpu.HBM)
    vmem = pl.BlockSpec(memory_space=pltpu.VMEM)
    dma = pltpu.SemaphoreType.DMA
    shapes = (
        jax.ShapeDtypeStruct((rows, cols), BF16),
        jax.ShapeDtypeStruct((shard, cols), F32),
        jax.ShapeDtypeStruct((1, shard), F32),
    )
    outs = pl.pallas_call(
        functools.partial(kernel, ny, nz),
        out_shape=shapes,
        in_specs=[hbm] * len(operands),
        out_specs=(vmem, vmem, vmem),
        scratch_shapes=[pltpu.VMEM(v.shape, v.dtype) for v in operands]
        + [
            pltpu.VMEM((shard, cols), BF16),
            pltpu.VMEM((2, shard, LANES), BF16),
            pltpu.VMEM((jn, slab, LANES), BF16),
            pltpu.VMEM((jn, 4, 2, slab, cols), BF16),
            pltpu.VMEM((jn, 4, 2, slab, cols), BF16),
            pltpu.VMEM((jn, 4, slab, cols), BF16),
            pltpu.VMEM((jn, 4, slab, cols), BF16),
            pltpu.VMEM((jn, plane - 1, slab, LANES), BF16),
            pltpu.VMEM((jn, 2, shard, LANES), BF16),
            pltpu.VMEM((steps, shard, LANES), BF16),
            pltpu.VMEM((shard, LANES), F32),
            pltpu.VMEM((plane, shard, LANES), F32),
            pltpu.VMEM((rows, cols), BF16),
            dma((len(operands),)),
            dma((2,)),
            dma((2,)),
            dma((3,)),
            dma((3,)),
            dma,
            dma((4,)),
            dma,
            dma((4,)),
            dma,
            dma((jn,)),
            dma,
            dma((jn,)),
            dma,
            dma,
            dma,
            dma,
            pltpu.SemaphoreType.REGULAR,
            pltpu.SemaphoreType.REGULAR,
        ],
        compiler_params=pltpu.CompilerParams(
            collective_id=0, has_side_effects=True, vmem_limit_bytes=40 * 2**20
        ),
        name="kv_exchange",
    )(*[pltpu.with_memory_space_constraint(v, pltpu.HBM) for v in operands])
    kv, wg, gg = pl.pallas_call(
        functools.partial(copy_kernel, len(outs)),
        out_shape=shapes,
        in_specs=[vmem] * len(outs),
        out_specs=(hbm, hbm, hbm),
        scratch_shapes=[dma((len(outs),))],
        name="kv_outputs",
    )(*[pltpu.with_memory_space_constraint(v, pltpu.VMEM) for v in outs])
    return (kv, wg, gg.reshape(-1))


def solution(mesh):
    ny = mesh.shape["dom"] // 4
    nz = mesh.shape["fsdp"] // 2
    return jax.shard_map(
        functools.partial(body, ny, nz),
        mesh=mesh,
        in_specs=(
            P(("dom", "fsdp"), None),
            P("fsdp"),
            P("fsdp", None),
            P(("dom", "fsdp")),
            P(("dom", "fsdp"), None),
            P(),
            P(),
        ),
        out_specs=(P(("dom", "fsdp"), None), P("fsdp", None), P("fsdp")),
        check_vma=False,
    )
```

```python
import functools

import jax
import jax.numpy as jnp
import numpy as np
from jax import lax
from jax.experimental import pallas as pl
from jax.experimental.pallas import tpu as pltpu
from jax.sharding import PartitionSpec as P

HD = 128
HALF = HD // 2
BLOCK = 128
LANES = 128
MESH = pl.DeviceIdType.MESH
F32 = jnp.float32
BF16 = jnp.bfloat16


def to_column(row, size):
    eye = lax.broadcasted_iota(jnp.int32, (size, size), 0) == lax.broadcasted_iota(
        jnp.int32, (size, size), 1
    )
    return jnp.sum(jnp.where(eye, row, jnp.float32(0.0)), axis=1, keepdims=True)


def to_row(column, size):
    eye = lax.broadcasted_iota(jnp.int32, (size, size), 0) == lax.broadcasted_iota(
        jnp.int32, (size, size), 1
    )
    return jnp.sum(jnp.where(eye, column, jnp.float32(0.0)), axis=0, keepdims=True)


def kernel(
    ny,
    nz,
    counts_hbm,
    ratios_hbm,
    gain_hbm,
    weight_hbm,
    positions_hbm,
    freq_hbm,
    tokens_hbm,
    cot_hbm,
    kv_ref,
    wg_ref,
    gg_ref,
    counts_ref,
    ratios_ref,
    gain_ref,
    weight_ref,
    positions_ref,
    freq_ref,
    tokens_ref,
    cot_ref,
    own_gw,
    land_g1,
    piece_g,
    full_gw,
    part_m,
    land_r0,
    sum_r0,
    land_r1,
    sum_r1,
    land_r2,
    sum_r2,
    land_r3,
    upstream,
    sem_in,
    sem_g1s,
    sem_g1r,
    sem_gxs,
    sem_gxr,
    sem_g2s,
    sem_g2r,
    sem_g3s,
    sem_g3r,
    sem_r0s,
    sem_r0r,
    sem_r1s,
    sem_r1r,
    sem_r2s,
    sem_r2r,
    sem_r3s,
    sem_r3r,
    sem_in_ring,
    sem_in_far,
):
    dom = lax.axis_index("dom")
    fsdp = lax.axis_index("fsdp")
    core = lax.rem(dom, 2)
    y = lax.rem(lax.div(dom, 2), ny)
    x_hi = lax.div(dom, 2 * ny)
    z = lax.div(fsdp, 2)
    x_lo = lax.rem(fsdp, 2)
    x = x_hi * 2 + x_lo
    q = x_hi * 2 + core
    jn = nz // 8
    plane = 4 * ny
    steps = 2 * jn
    rows, width = tokens_ref.shape
    shard, cols = weight_ref.shape
    slab = 2 * shard
    key_width = cols // 2
    heads = key_width // HD
    group = 8 * slab
    lo_own = lax.rem(z + core, 2)
    lo_sib = 1 - lo_own

    def dev(xx, yy, cc, zz):
        return (lax.div(xx, 2) * (2 * ny) + yy * 2 + cc, zz * 2 + lax.rem(xx, 2))

    def remote(src, dst, send, recv, device):
        return pltpu.make_async_remote_copy(
            src_ref=src,
            dst_ref=dst,
            send_sem=send,
            recv_sem=recv,
            device_id=device,
            device_id_type=MESH,
        )

    def lane_tile(i):
        return pl.ds(pl.multiple_of(i * LANES, LANES), LANES)

    def wrap_z(value):
        return lax.rem(value + 2 * nz, nz)

    loads = [
        pltpu.make_async_copy(src, dst, sem_in.at[i])
        for i, (src, dst) in enumerate(
            (
                (tokens_hbm, tokens_ref),
                (cot_hbm, cot_ref),
                (positions_hbm, positions_ref),
                (freq_hbm, freq_ref),
                (weight_hbm, weight_ref),
                (gain_hbm, gain_ref),
                (counts_hbm, counts_ref),
                (ratios_hbm, ratios_ref),
            )
        )
    ]
    for load in loads:
        load.start()

    own_class = q + 4 * x_lo
    own_shift = q - 4 * x_lo
    residue = lax.rem(z - own_class + 2 * nz, 8)
    hi_own = lax.div(residue, 2)
    home = lax.div(wrap_z(z - own_shift), 8)

    barrier = pltpu.get_barrier_semaphore()

    def greet(device):
        pl.semaphore_signal(barrier, inc=1, device_id=device, device_id_type=MESH)

    xs = [lax.rem(x + i, 4) for i in range(4)]
    ys = [lax.rem(y + i, ny) for i in range(ny)]

    def class_of(xx, cc):
        return lax.div(xx, 2) * 2 + cc + 4 * lax.rem(xx, 2)

    def hi_of(xx, cc):
        return lax.div(lax.rem(z - class_of(xx, cc) + 2 * nz, 8), 2)

    his = [hi_of(xx, core) for xx in xs]
    at_plane = [[dev(xx, yy, core, z) for yy in ys] for xx in xs]
    at_other = [[(a + 1 - 2 * core, b) for a, b in line] for line in at_plane]
    sibling = at_other[0][0]
    peers = [(i, j) for i in range(4) for j in range(ny)][1:]
    peers.sort(key=lambda p: (-min(p[0], 4 - p[0]) - min(p[1], ny - p[1]), sum(p)))

    greet(sibling)
    for i, j in peers:
        greet(at_plane[i][j])
        if i % 2 == 0:
            greet(at_other[i][j])
    near_self = (own_class == 0).astype(jnp.int32)
    for half in range(2):
        owner = dev(x_hi * 2 + half, y, core, wrap_z(z - own_shift))
        if half == 0:

            @pl.when(own_class != 0)
            def _(owner=owner):
                greet(owner)

        else:
            greet(owner)
    for t in range(2):
        near = dev(x_hi * 2 + t, y, core, wrap_z(z + q - 4 * t))
        if t == 0:

            @pl.when(own_class != 0)
            def _(near=near):
                greet(near)

        else:
            greet(near)
    ring = min(jn - 1, 2)
    ahead = dev(x, y, core, wrap_z(z + 8))
    behind = dev(x, y, core, wrap_z(z - 8))
    if jn > 1:
        greet(ahead)
    if jn > 2:
        greet(behind)

    loads[4].wait()
    loads[5].wait()
    gain_col = to_column(gain_ref[...].astype(F32), shard)
    weight = weight_ref[...].astype(F32)
    own_gw[...] = (weight * gain_col).astype(BF16)

    loads[2].wait()
    loads[3].wait()
    pos = positions_ref[...].astype(F32)
    pos_col = jnp.concatenate(
        [to_column(pos[i : i + 1, :], LANES) for i in range(rows // LANES)], axis=0
    )
    angles = pos_col * freq_ref[...]
    cosines = jnp.cos(angles)
    lane_ids = lax.broadcasted_iota(jnp.int32, (rows, HD), 1)
    sines = jnp.where(lane_ids < HALF, -1.0, 1.0) * jnp.sin(angles)

    loads[6].wait()
    loads[7].wait()
    counts = counts_ref[...].astype(F32)
    n_dom, n_mem = counts.shape
    domain_rows = BLOCK * jnp.sum(counts, axis=1, keepdims=True)
    live_total = jnp.sum(domain_rows, axis=0, keepdims=True)
    ratio = to_column(ratios_ref[...].astype(F32), n_dom)
    factor = ratio / jnp.sum(ratio, axis=0, keepdims=True) * live_total / domain_rows
    dom_ids = lax.broadcasted_iota(jnp.int32, (n_dom, 1), 0)
    own_factor = jnp.sum(jnp.where(dom_ids == dom, factor, 0.0), axis=0, keepdims=True)
    at_dom = lax.broadcasted_iota(jnp.int32, (n_dom, n_mem), 0) == dom
    at_mem = lax.broadcasted_iota(jnp.int32, (n_dom, n_mem), 1) == fsdp
    own_count = jnp.sum(
        jnp.sum(jnp.where(at_dom & at_mem, counts, 0.0), axis=1, keepdims=True),
        axis=0,
        keepdims=True,
    )
    row_ids = lax.broadcasted_iota(jnp.int32, (rows, 1), 0).astype(F32)
    row_factor = jnp.where(row_ids < BLOCK * own_count, own_factor, 0.0)

    loads[0].wait()
    token = tokens_ref[...].astype(F32)
    mean_square = jnp.sum(token * token, axis=1, keepdims=True) * (1.0 / width)
    inv_norm = lax.rsqrt(mean_square + 1e-06)

    loads[1].wait()
    scale = row_factor * inv_norm
    for h in range(2 * heads):
        part = cot_ref[:, h * HD : (h + 1) * HD].astype(F32) * scale
        if h < heads:
            part = part * cosines - pltpu.roll(part, HALF, 1) * sines
        upstream[:, h * HD : (h + 1) * HD] = part.astype(BF16)

    pl.semaphore_wait(barrier, plane + plane // 2 - 1 + 4 + ring - 2 * near_self)

    def tell(sem, device):
        pl.semaphore_signal(sem, inc=1, device_id=device, device_id_type=MESH)

    if jn > 1:
        tell(sem_in_ring, ahead)
    if jn > 2:
        tell(sem_in_ring, behind)

    def g1_copy(t):
        return remote(
            own_gw.at[:, lane_tile(y)],
            land_g1.at[x_lo],
            sem_g1s.at[t],
            sem_g1r.at[x_lo],
            dev(x_hi * 2 + t, y, core, wrap_z(z + q - 4 * t)),
        )

    g1_local = pltpu.make_async_copy(
        own_gw.at[:, lane_tile(y)], land_g1.at[0], sem_g1r.at[0]
    )

    @pl.when(own_class != 0)
    def _():
        g1_copy(0).start()

    @pl.when(own_class == 0)
    def _():
        g1_local.start()

    g1_copy(1).start()

    def r0_copy(j):
        return remote(
            part_m.at[j, :, lo_sib], land_r0.at[j], sem_r0s, sem_r0r.at[j], sibling
        )

    def m_step(j, carry):
        lhs = tokens_ref[:, pl.ds(pl.multiple_of(j * group, group), group)]
        prod = lax.dot_general(
            lhs, upstream[...], (((0,), (0,)), ((), ())), preferred_element_type=F32
        )
        part_m[j] = prod.reshape(4, 2, slab, cols).astype(BF16)
        r0_copy(j).start()
        return carry

    def r1_send(j, carry):
        r0_copy(j).wait_recv()
        total = part_m[j, :, lo_own].astype(F32) + land_r0[j].astype(F32)
        sum_r0[j] = total.astype(BF16)
        for k, (dx, dy) in enumerate(peers):
            remote(
                sum_r0.at[j, his[dx], :, lane_tile(ys[dy])],
                land_r1.at[j, k],
                sem_r1s,
                sem_r1r.at[j],
                at_plane[dx][dy],
            ).start()
        return carry

    m_step(0, 0)

    def m_and_r1(j, carry):
        m_step(j, carry)
        return r1_send(j - 1, carry)

    lax.fori_loop(1, jn, m_and_r1, 0)

    for half in range(2):
        pltpu.make_async_copy(
            land_g1.at[half], land_g1.at[half], sem_g1r.at[half]
        ).wait()
    piece_g[home] = jnp.concatenate(
        [land_g1[0].astype(F32), land_g1[1].astype(F32)], axis=0
    ).astype(BF16)

    def ring_copy(i, at, device):
        return remote(
            piece_g.at[at], piece_g.at[at], sem_gxs.at[i], sem_gxr.at[i], device
        )

    def nth(i):
        return lax.rem(home + i + 2 * jn, jn)

    if jn > 1:
        ring_copy(0, home, ahead).start()
    if jn > 2:
        ring_copy(1, home, behind).start()

    r1_send(jn - 1, 0)
    if jn > 1:
        pl.semaphore_wait(sem_in_ring, ring)
    if jn > 3:
        tell(sem_in_far, ahead)

    def arrived(buffer, sem):
        pltpu.make_async_copy(buffer, buffer, sem).wait()

    def r1_arrive(j, carry):
        arrived(land_r1.at[j], sem_r1r.at[j])
        total = sum_r0[j, hi_own, :, lane_tile(y)].astype(F32)
        for k in range(plane - 1):
            total = total + land_r1[j, k].astype(F32)
        for half in range(2):
            sum_r1[j, half] = total[half * shard : (half + 1) * shard, :].astype(BF16)
        return carry

    def r2_copy(j, half):
        far = 8 * j + residue
        slot = 2 * lax.div(wrap_z(z - own_class - far), 8) + x_lo
        return remote(
            sum_r1.at[j, half],
            land_r2.at[slot],
            sem_r2s,
            sem_r2r,
            dev(x_hi * 2 + half, y, core, far),
        )

    def r2_send(j, carry):
        stays = (own_class == 0) & (j == home)

        @pl.when(jnp.logical_not(stays))
        def _():
            r2_copy(j, 0).start()

        @pl.when(stays)
        def _():
            pltpu.make_async_copy(sum_r1.at[j, 0], land_r2.at[0], sem_r2r).start()

        r2_copy(j, 1).start()
        return carry

    def r1_and_r2(j, carry):
        r1_arrive(j, carry)
        return r2_send(j, carry)

    early = min(2, jn)
    lax.fori_loop(0, early, r1_arrive, 0)
    if jn > 1:
        ring_copy(0, nth(-1), behind).wait_recv()
    if jn > 3:
        ring_copy(2, nth(-1), ahead).start()
        pl.semaphore_wait(sem_in_far, 1)
    lax.fori_loop(0, early, r2_send, 0)
    lax.fori_loop(early, jn, r1_and_r2, 0)
    def g2_send(i):
        at = nth(i)
        view = full_gw.at[at, hi_own, lo_own, :, lane_tile(y)]
        for dx, dy in peers:
            remote(
                piece_g.at[at], view, sem_g2s, sem_g2r.at[dx], at_plane[dx][dy]
            ).start()
        pltpu.make_async_copy(piece_g.at[at], view, sem_g2r.at[0]).start()

    g2_send(0)
    if jn > 1:
        g2_send(-1)
    if jn > 2:
        ring_copy(1, nth(1), ahead).wait_recv()
        g2_send(1)
    if jn > 3:
        ring_copy(2, nth(2), behind).wait_recv()
        g2_send(2)

    arrived(land_r0, sem_r0s)
    arrived(land_r1, sem_r1s)

    @pl.when(own_class != 0)
    def _():
        g1_copy(0).wait_send()

    g1_copy(1).wait_send()
    for i in range(min(jn - 1, 3)):
        ring_copy(i, home, ahead).wait_send()

    arrived(land_r2, sem_r2r)
    total2 = land_r2[0].astype(F32)
    for s in range(1, steps):
        total2 = total2 + land_r2[s].astype(F32)
    sum_r2[...] = total2

    slot3 = 4 * y + q
    pltpu.make_async_copy(sum_r2, land_r3.at[slot3], sem_r3r).start()

    def r3_send(device):
        remote(sum_r2, land_r3.at[slot3], sem_r3s, sem_r3r, device).start()

    r3_send(sibling)
    for dx in (0, 2):
        for dy in range(ny):
            if dx or dy:
                r3_send(at_plane[dx][dy])
                r3_send(at_other[dx][dy])

    def g3_copy(hi, lo, i):
        view = full_gw.at[:, hi, lo]
        return remote(view, view, sem_g3s, sem_g3r.at[i], sibling)

    for dx in range(4):
        back = (4 - dx) % 4
        arrived(full_gw.at[:, his[back], lo_own], sem_g2r.at[dx])
        g3_copy(his[back], lo_own, dx).start()

    for dx in range(4):
        back = (4 - dx) % 4
        arrived(full_gw.at[:, hi_of(xs[back], 1 - core), lo_sib], sem_g3r.at[dx])

    pair = 2 * LANES
    for i in range(cols // pair):
        rhs = full_gw[:, :, :, :, i * pair : (i + 1) * pair].reshape(width, pair)
        projected = jnp.dot(tokens_ref[...], rhs, preferred_element_type=F32)
        projected = projected * inv_norm
        for h in range(pair // HD):
            part = projected[:, h * HD : (h + 1) * HD]
            if i * (pair // HD) + h < heads:
                part = part * cosines + pltpu.roll(part, HALF, 1) * sines
            at = i * pair + h * HD
            kv_ref[:, at : at + HD] = part.astype(BF16)

    arrived(land_r3, sem_r3r)
    root = jnp.sqrt(live_total)
    gain_sum = jnp.zeros((shard, 1), F32)
    for i in range(ny):
        tile = slice(i * LANES, (i + 1) * LANES)
        total3 = land_r3[4 * i] + land_r3[4 * i + 1] + land_r3[4 * i + 2] + land_r3[4 * i + 3]
        wg_ref[:, tile] = total3 * gain_col / root
        gain_sum = gain_sum + jnp.sum(total3 * weight[:, tile], axis=1, keepdims=True)
    gg_ref[...] = to_row(gain_sum / root, shard)

    arrived(land_r1, sem_g2s)
    arrived(full_gw.at[:, :, lo_own], sem_g3s)

    @pl.when(own_class != 0)
    def _():
        arrived(land_r2, sem_r2s)

    @pl.when(own_class == 0)
    def _():
        arrived(land_r2.at[pl.ds(0, steps - 1)], sem_r2s)

    arrived(land_r3.at[pl.ds(0, plane - 1)], sem_r3s)


def copy_kernel(count, *refs):
    sems = refs[-1]
    copies = [
        pltpu.make_async_copy(refs[i], refs[count + i], sems.at[i])
        for i in range(count)
    ]
    for copy in copies:
        copy.start()
    for copy in copies:
        copy.wait()


def body(ny, nz, tokens, gain, kv_weight, positions, cotangent, counts, ratios):
    rows, width = tokens.shape
    shard, cols = kv_weight.shape
    jn, plane = nz // 8, 4 * ny
    steps = 2 * jn
    slab = 2 * shard
    exponents = np.arange(HALF) * (2.0 / HD)
    freq = np.power(1000000.0, -exponents).astype(np.float32)
    freq = jnp.asarray(np.concatenate([freq, freq])[None, :])
    operands = (
        counts,
        ratios.reshape(1, -1),
        gain.reshape(1, -1),
        kv_weight,
        positions.reshape(-1, LANES),
        freq,
        tokens,
        cotangent,
    )
    hbm = pl.BlockSpec(memory_space=pltpu.HBM)
    vmem = pl.BlockSpec(memory_space=pltpu.VMEM)
    dma = pltpu.SemaphoreType.DMA
    shapes = (
        jax.ShapeDtypeStruct((rows, cols), BF16),
        jax.ShapeDtypeStruct((shard, cols), F32),
        jax.ShapeDtypeStruct((1, shard), F32),
    )
    outs = pl.pallas_call(
        functools.partial(kernel, ny, nz),
        out_shape=shapes,
        in_specs=[hbm] * len(operands),
        out_specs=(vmem, vmem, vmem),
        scratch_shapes=[pltpu.VMEM(v.shape, v.dtype) for v in operands]
        + [
            pltpu.VMEM((shard, cols), BF16),
            pltpu.VMEM((2, shard, LANES), BF16),
            pltpu.VMEM((jn, slab, LANES), BF16),
            pltpu.VMEM((jn, 4, 2, slab, cols), BF16),
            pltpu.VMEM((jn, 4, 2, slab, cols), BF16),
            pltpu.VMEM((jn, 4, slab, cols), BF16),
            pltpu.VMEM((jn, 4, slab, cols), BF16),
            pltpu.VMEM((jn, plane - 1, slab, LANES), BF16),
            pltpu.VMEM((jn, 2, shard, LANES), BF16),
            pltpu.VMEM((steps, shard, LANES), BF16),
            pltpu.VMEM((shard, LANES), F32),
            pltpu.VMEM((plane, shard, LANES), F32),
            pltpu.VMEM((rows, cols), BF16),
            dma((len(operands),)),
            dma((2,)),
            dma((2,)),
            dma((3,)),
            dma((3,)),
            dma,
            dma((4,)),
            dma,
            dma((4,)),
            dma,
            dma((jn,)),
            dma,
            dma((jn,)),
            dma,
            dma,
            dma,
            dma,
            pltpu.SemaphoreType.REGULAR,
            pltpu.SemaphoreType.REGULAR,
        ],
        compiler_params=pltpu.CompilerParams(
            collective_id=0, has_side_effects=True, vmem_limit_bytes=40 * 2**20
        ),
        name="kv_exchange",
    )(*[pltpu.with_memory_space_constraint(v, pltpu.HBM) for v in operands])
    kv, wg, gg = pl.pallas_call(
        functools.partial(copy_kernel, len(outs)),
        out_shape=shapes,
        in_specs=[vmem] * len(outs),
        out_specs=(hbm, hbm, hbm),
        scratch_shapes=[dma((len(outs),))],
        name="kv_outputs",
    )(*[pltpu.with_memory_space_constraint(v, pltpu.VMEM) for v in outs])
    return (kv, wg, gg.reshape(-1))


def solution(mesh):
    ny = mesh.shape["dom"] // 4
    nz = mesh.shape["fsdp"] // 2
    return jax.shard_map(
        functools.partial(body, ny, nz),
        mesh=mesh,
        in_specs=(
            P(("dom", "fsdp"), None),
            P("fsdp"),
            P("fsdp", None),
            P(("dom", "fsdp")),
            P(("dom", "fsdp"), None),
            P(),
            P(),
        ),
        out_specs=(P(("dom", "fsdp"), None), P("fsdp", None), P("fsdp")),
        check_vma=False,
    )
```
